512 devices in a mesh: head: 4 (over y), tok: 128 (over z, x, core).
Axes of the slice: x: 4, y: 4, z: 16, core: 2. Of those that a mesh axis runs over, the one named last changes fastest.
Arguments:
- query_input: bfloat16 [32768, 2048], P('tok', 'head'), may hold values from -6 to 6
- key_input: bfloat16 [32768, 2048], P('tok', 'head'), may hold values from -6 to 6
- value_input: bfloat16 [32768, 2048], P('tok', 'head'), may hold values from -6 to 6
- out_grad: bfloat16 [32768, 2048], P('tok', 'head'), may hold values from -0.4453125 to 0.4453125
- token_rates: float32 [32768, 4], P('tok', 'head'), may hold values from 0.00022097086 to 0.0022097088
- out_gain: float32 [2048], P('head'), may hold values from 0.1 to 1.9
- gate_prior: bfloat16 [4, 512, 256], P('head'), may hold values from -0.8242256 to 0.8242256
- up_prior: bfloat16 [4, 512, 256], P('head'), may hold values from -0.8242256 to 0.8242256
- down_prior: bfloat16 [4, 256, 512], P('head'), may hold values from -3.496893 to 3.496893
Outputs:
- query_grad: bfloat16 [32768, 2048], P('tok', 'head')
- key_grad: bfloat16 [32768, 2048], P('tok', 'head')
- value_grad: bfloat16 [32768, 2048], P('tok', 'head')
- gate_prior_grad: float32 [4, 512, 256], P('head', None, 'tok')
- up_prior_grad: float32 [4, 512, 256], P('head', None, 'tok')
- down_prior_grad: float32 [4, 256, 512], P('head', None, 'tok')
The draws below stay inside these ranges and needn't reach their ends.
All inputs are finite; a program needn't handle non-finite values.
Results may differ from the reference program's by a relative error of at most 0.014.
Values may be sent and summed in bfloat16 or wider, within the bound.
A program may use at most 64 MiB of HBM per device.

```python
import math
import jax
import jax.numpy as jnp
from jax import lax

DH = 512
FH = 256
HEADS = 4
WIDTH = 2048
TOKENS = 32768


def scaled_weight(base_key, row_count, col_count, fan_in, head_rise):
    draw_key, row_key, col_key = jax.random.split(base_key, 3)
    base_draw = jnp.clip(jax.random.normal(draw_key, (HEADS, row_count, col_count), jnp.float32), -4.0, 4.0)
    row_scale = jnp.exp(jax.random.uniform(row_key, (HEADS, row_count, 1), jnp.float32, -1.15, 1.15))
    col_scale = jnp.exp(jax.random.uniform(col_key, (HEADS, 1, col_count), jnp.float32, -1.15, 1.15))
    head_scale = head_rise ** (jnp.arange(HEADS, dtype=jnp.float32) / max(HEADS - 1, 1))
    return base_draw * row_scale * col_scale * head_scale[:, None, None] / jnp.sqrt(4.6 * fan_in)


def draw_gate_prior(key, part):
    return scaled_weight(jax.random.fold_in(key, 101), DH, FH, DH, 1.0).astype(jnp.bfloat16)


def draw_up_prior(key, part):
    return scaled_weight(jax.random.fold_in(key, 202), DH, FH, DH, 1.0).astype(jnp.bfloat16)


def draw_down_prior(key, part):
    return scaled_weight(jax.random.fold_in(key, 303), FH, DH, FH, 3.0).astype(jnp.bfloat16)


def levels(stream_key, dims, pieces, low, top_value):
    level, own = 1.0, jax.random.fold_in(stream_key, 6)
    for axis_at, parts in pieces:
        draws = jnp.exp(jax.random.uniform(jax.random.fold_in(own, axis_at), (parts,), jnp.float32, low / len(pieces), top_value / len(pieces)))
        level = level * jnp.repeat(draws, dims[axis_at] // parts).reshape([-1 if axis == axis_at else 1 for axis in range(len(dims))])
    return level


def normal_values(rng, dims, spread, reach, shards=(), held_as=jnp.bfloat16):
    array = jax.random.normal(rng, dims, jnp.float32) * spread
    if len(shards) > 0:
        array = levels(rng, dims, shards, -0.22, 0.18) * array
    return jnp.clip(array, min=-reach, max=reach).astype(held_as)


def setup_inputs(seed: int = 0) -> dict:
    keys = jax.random.split(jax.random.key(seed), 10)
    return {
        "query_input": normal_values(keys[0], (TOKENS, WIDTH), 1.0, 6.0, ((0, 128), (1, 4))),
        "key_input": normal_values(keys[1], (TOKENS, WIDTH), 1.0, 6.0, ((0, 128), (1, 4))),
        "value_input": normal_values(keys[2], (TOKENS, WIDTH), 1.0, 6.0, ((0, 128), (1, 4))),
        "out_grad": normal_values(keys[3], (TOKENS, WIDTH), (TOKENS ** -0.25), 0.4453125, ((0, 128), (1, 4))),
        "token_rates": jnp.clip(jnp.exp(math.log(0.0022097088) - 2.3025852 * jax.random.uniform(keys[4], (TOKENS, HEADS), jnp.float32) ** levels(keys[4], (TOKENS, HEADS), ((0, 128), (1, 4)), -0.2, 0.2)), 0.00022097086, 0.0022097088),
        "out_gain": jnp.clip(1.0 + 0.18 * jax.random.normal(keys[5], (WIDTH,), jnp.float32), 0.1, 1.9),
        "gate_prior": draw_gate_prior(jax.random.fold_in(keys[9], 71), 0),
        "up_prior": draw_up_prior(jax.random.fold_in(keys[9], 71), 0),
        "down_prior": draw_down_prior(jax.random.fold_in(keys[9], 71), 0),
    }


EPSILON = 1e-06

def matmul(first_op, second_op):
    return jnp.dot(first_op, second_op, preferred_element_type=jnp.float32)

def contract_rows(first_op, second_op):
    return lax.dot_general(first_op, second_op, (((0,), (0,)), ((), ())), preferred_element_type=jnp.float32)

def contract_cols(first_op, second_op):
    return lax.dot_general(first_op, second_op, (((1,), (1,)), ((), ())), preferred_element_type=jnp.float32)

def silu_parts(hidden):
    sigmoid_value = jax.nn.sigmoid(hidden)
    silu_value = hidden * sigmoid_value
    silu_slope = sigmoid_value * (1.0 + hidden * (1.0 - sigmoid_value))
    curvature = sigmoid_value * (1.0 - sigmoid_value) * (2.0 + hidden * (1.0 - 2.0 * sigmoid_value))
    return (silu_value, silu_slope, curvature)

def update_forward(key_head, value_head, rate_head, priors):
    gate_weight, up_weight, down_weight = priors
    gate_pre = matmul(key_head, gate_weight)
    up_pre = matmul(key_head, up_weight)
    silu_value, silu_slope, curvature = silu_parts(gate_pre)
    mixed_act = (silu_value * up_pre).astype(jnp.bfloat16)
    value_push = (-rate_head[:, None] * value_head.astype(jnp.float32)).astype(jnp.bfloat16)
    down_update = contract_rows(mixed_act, value_push)
    down_back = contract_cols(value_push, down_weight)
    gate_back = (down_back * up_pre * silu_slope).astype(jnp.bfloat16)
    up_back = (down_back * silu_value).astype(jnp.bfloat16)
    gate_update = contract_rows(key_head, gate_back)
    up_update = contract_rows(key_head, up_back)
    update_saved = (up_pre, silu_value, silu_slope, curvature, mixed_act, value_push, down_back, gate_back, up_back)
    return ((gate_update, up_update, down_update), update_saved)

def renormalize(prior, update):
    prior_f = prior.astype(jnp.float32)
    moved_weight = prior_f - update
    prior_norm = jnp.sqrt(lax.optimization_barrier(jnp.sum(prior_f * prior_f, axis=0)) + EPSILON)
    moved_norm = jnp.sqrt(lax.optimization_barrier(jnp.sum(moved_weight * moved_weight, axis=0)) + EPSILON)
    return (moved_weight, prior_norm, moved_norm)

def apply_forward(query_head, fast_weights):
    gate_pre = matmul(query_head, fast_weights[0])
    up_pre = matmul(query_head, fast_weights[1])
    silu_value, silu_slope, curvature = silu_parts(gate_pre)
    mixed_act = (silu_value * up_pre).astype(jnp.bfloat16)
    output = matmul(mixed_act, fast_weights[2])
    return (output, (up_pre, silu_value, silu_slope, mixed_act))

def apply_backward(query_head, fast_weights, apply_saved, out_back):
    up_pre, silu_value, silu_slope, mixed_act = apply_saved
    down_grad = contract_rows(mixed_act, out_back)
    mixed_back = contract_cols(out_back, fast_weights[2])
    gate_back = (mixed_back * up_pre * silu_slope).astype(jnp.bfloat16)
    up_back = (mixed_back * silu_value).astype(jnp.bfloat16)
    gate_grad = contract_rows(query_head, gate_back)
    up_grad = contract_rows(query_head, up_back)
    query_back = (contract_cols(gate_back, fast_weights[0]) + contract_cols(up_back, fast_weights[1])).astype(jnp.bfloat16)
    return ((gate_grad, up_grad, down_grad), query_back)

def norm_adjoint(prior, moved_weight, prior_norm, moved_norm, fast_grad, column_dot):
    moved_grad = prior_norm / moved_norm * (fast_grad - moved_weight * (column_dot / (moved_norm * moved_norm)))
    direct = prior.astype(jnp.float32) * (column_dot / (moved_norm * prior_norm))
    return (moved_grad, direct)

def second_adjoint(key_head, rate_head, priors, update_saved, cotangent):
    gate_weight, up_weight, down_weight = priors
    up_pre, silu_value, silu_slope, curvature, mixed_act, value_push, down_back, gate_back, up_back = update_saved
    gate_cot, up_cot, down_cot = cotangent
    gate_bar = matmul(key_head, gate_cot)
    up_bar = matmul(key_head, up_cot)
    mixed_bar = contract_cols(value_push, down_cot)
    push_bar = matmul(mixed_act, down_cot)
    down_back_bar = (gate_bar * up_pre * silu_slope + up_bar * silu_value).astype(jnp.bfloat16)
    up_pre_bar = (gate_bar * down_back * silu_slope + mixed_bar * silu_value).astype(jnp.bfloat16)
    gate_pre_bar = ((up_bar * down_back + mixed_bar * up_pre) * silu_slope + gate_bar * down_back * up_pre * curvature).astype(jnp.bfloat16)
    down_prior_bar = contract_rows(down_back_bar, value_push)
    gate_prior_bar = contract_rows(key_head, gate_pre_bar)
    up_prior_bar = contract_rows(key_head, up_pre_bar)
    value_grad = (rate_head[:, None] * (push_bar + matmul(down_back_bar, down_weight))).astype(jnp.bfloat16)
    key_total = contract_cols(gate_back, gate_cot) + contract_cols(up_back, up_cot) + contract_cols(gate_pre_bar, gate_weight) + contract_cols(up_pre_bar, up_weight)
    key_grad = (-key_total).astype(jnp.bfloat16)
    return ((gate_prior_bar, up_prior_bar, down_prior_bar), key_grad, value_grad)

def reference(query_input, key_input, value_input, out_grad, token_rates, out_gain, gate_prior, up_prior, down_prior):
    head_states = []
    outputs = []
    for head_index in range(HEADS):
        lower = head_index * DH
        key_head = key_input[:, lower:lower + DH]
        value_head = value_input[:, lower:lower + DH]
        query_head = query_input[:, lower:lower + DH]
        rate_head = token_rates[:, head_index]
        priors = (gate_prior[head_index], up_prior[head_index], down_prior[head_index])
        updates, update_saved = update_forward(key_head, value_head, rate_head, priors)
        renormed = [renormalize(priors[matrix_index], updates[matrix_index]) for matrix_index in range(3)]
        fast_weights = tuple(((moved_weight * (prior_norm / moved_norm)).astype(jnp.bfloat16) for moved_weight, prior_norm, moved_norm in renormed))
        output, apply_saved = apply_forward(query_head, fast_weights)
        outputs.append(output)
        head_states.append((key_head, query_head, rate_head, priors, update_saved, renormed, fast_weights, apply_saved))
    output_all = jnp.concatenate(outputs, axis=1)
    gain_weighted = out_grad.astype(jnp.float32) * out_gain
    square_sum = lax.optimization_barrier(jnp.sum(output_all * output_all, axis=1))
    dot_sum = lax.optimization_barrier(jnp.sum(gain_weighted * output_all, axis=1))
    inverse = lax.rsqrt(square_sum / WIDTH + EPSILON)
    out_back_all = (inverse[:, None] * gain_weighted - output_all * (inverse * inverse * inverse * dot_sum / WIDTH)[:, None]).astype(jnp.bfloat16)
    query_grads, key_grads, value_grads = ([], [], [])
    gate_grads, up_grads, down_grads = ([], [], [])
    for head_index in range(HEADS):
        key_head, query_head, rate_head, priors, update_saved, renormed, fast_weights, apply_saved = head_states[head_index]
        lower = head_index * DH
        fast_grads, query_back = apply_backward(query_head, fast_weights, apply_saved, out_back_all[:, lower:lower + DH])
        cotangent = []
        global_parts = []
        for matrix_index in range(3):
            moved_weight, prior_norm, moved_norm = renormed[matrix_index]
            column_dot = lax.optimization_barrier(jnp.sum(fast_grads[matrix_index] * moved_weight, axis=0))
            moved_grad, direct = norm_adjoint(priors[matrix_index], moved_weight, prior_norm, moved_norm, fast_grads[matrix_index], column_dot)
            cotangent.append(moved_grad.astype(jnp.bfloat16))
            global_parts.append(moved_grad + direct)
        prior_bars, key_grad, value_grad = second_adjoint(key_head, rate_head, priors, update_saved, tuple(cotangent))
        query_grads.append(query_back)
        key_grads.append(key_grad)
        value_grads.append(value_grad)
        gate_grads.append(global_parts[0] - prior_bars[0])
        up_grads.append(global_parts[1] - prior_bars[1])
        down_grads.append(global_parts[2] - prior_bars[2])
    return (jnp.concatenate(query_grads, axis=1), jnp.concatenate(key_grads, axis=1), jnp.concatenate(value_grads, axis=1), jnp.stack(gate_grads), jnp.stack(up_grads), jnp.stack(down_grads))
```

```python
import jax
import jax.numpy as jnp
from jax import lax
from jax.experimental import pallas as pl
from jax.experimental.pallas import tpu as pltpu
from jax.sharding import PartitionSpec as P

EPSILON = 1e-06
CORES = 2
XS = 4
LANE = 128
BF = jnp.bfloat16
F32 = jnp.float32
MESH = pl.DeviceIdType.MESH
PIECES = ((0,), (1, 2))


def nn(a, b):
    return lax.dot_general(a, b, (((1,), (0,)), ((), ())), preferred_element_type=F32)


def nt(a, b):
    return lax.dot_general(a, b, (((1,), (1,)), ((), ())), preferred_element_type=F32)


def tn(a, b):
    return lax.dot_general(a, b, (((0,), (0,)), ((), ())), preferred_element_type=F32)


def log2(n):
    return n.bit_length() - 1


class Layout:
    def __init__(self, n, zs):
        self.n, self.zs = n, zs
        self.r = n // (CORES * XS * zs)
        self.rows = self.r * zs

    def natural(self, pos):
        lz, lr, lx, lc = log2(self.zs), log2(self.r), log2(XS), log2(CORES)
        z = pos & (self.zs - 1)
        r = lax.shift_right_logical(pos, lz) & (self.r - 1)
        x = lax.shift_right_logical(pos, lz + lr) & (XS - 1)
        c = lax.shift_right_logical(pos, lz + lr + lx) & (CORES - 1)
        return (z << (lx + lc + lr)) | (x << (lc + lr)) | (c << lr) | r

    def onehot(self):
        shape = (self.n, self.n)
        rows = lax.broadcasted_iota(jnp.int32, shape, 0)
        cols = self.natural(lax.broadcasted_iota(jnp.int32, shape, 1))
        return jnp.where(rows == cols, 1.0, 0.0).astype(BF)

    def onehot_t(self):
        shape = (self.n, self.n)
        rows = self.natural(lax.broadcasted_iota(jnp.int32, shape, 0))
        cols = lax.broadcasted_iota(jnp.int32, shape, 1)
        return jnp.where(rows == cols, 1.0, 0.0).astype(BF)


def body(heads, toks, q_ref, k_ref, v_ref, g_ref, rate_ref, gain_ref, w1_ref, w3_ref, w2_ref,
         qo_ref, ko_ref, vo_ref, own_ref, s):
    T, DH = q_ref.shape
    FH = w1_ref.shape[1]
    Z = toks // (CORES * XS)
    BR = DH * FH // (CORES * XS * LANE)
    NS = BR // Z
    fl, dl = Layout(FH, Z), Layout(DH, Z)
    layouts = (dl, fl, fl)
    JS = (FH // LANE, DH // LANE, DH // LANE)
    h = lax.axis_index("head")
    t = lax.axis_index("tok")
    c = lax.rem(t, CORES)
    x = lax.rem(t // CORES, XS)
    z = t // (CORES * XS)

    def at(c_, x_, z_):
        return (h, (z_ * XS + x_) * CORES + c_)

    other = at(1 - c, x, z)

    def x_peer(k):
        return lax.rem(x + k, XS)

    def z_peer(k):
        return lax.rem(z + k, Z)

    def head_peer(k):
        return lax.rem(h + k, heads)

    def z_step(i):
        half = (i + 1) // 2
        return Z // 2 + jnp.where(lax.rem(i, 2) == 0, half, -half)

    x_order = sorted(range(1, XS), key=lambda k: -min(k, XS - k))

    barrier = pltpu.get_barrier_semaphore()
    pl.semaphore_signal(barrier, inc=1, device_id=other, device_id_type=MESH)
    for k in range(1, XS):
        pl.semaphore_signal(barrier, inc=1, device_id=at(c, x_peer(k), z), device_id_type=MESH)

    def greet_z(k, carry):
        pl.semaphore_signal(barrier, inc=1, device_id=at(c, x, z_peer(k)), device_id_type=MESH)
        return carry

    lax.fori_loop(1, Z, greet_z, 0)
    for k in range(1, heads):
        pl.semaphore_signal(barrier, inc=1, device_id=(head_peer(k), t), device_id_type=MESH)

    RC = min(32, T)

    def each_rows(fn):
        def step(i, carry):
            fn(pl.ds(pl.multiple_of(i * RC, RC), RC))
            return carry

        lax.fori_loop(0, T // RC, step, 0)

    def remote(src, dst, send, recv, device):
        return pltpu.make_async_remote_copy(
            src_ref=src, dst_ref=dst, send_sem=send, recv_sem=recv, device_id=device, device_id_type=MESH
        )

    def wide(v, n):
        return jnp.concatenate([v] * (n // LANE), axis=1)

    def column(row):
        return jnp.broadcast_to(row, (LANE, row.shape[1])).T

    def parts(hidden):
        sg = jax.nn.sigmoid(hidden)
        return sg, hidden * sg, sg * (1.0 + hidden * (1.0 - sg))

    def put(ph, m, val):
        pc, mi = s.place[m]
        lay, js = layouts[m], JS[m]
        ref = s.sb[ph][pc]
        for cx in range(CORES * XS):
            for j in range(js):
                lo = mi * BR + j * lay.rows
                ref[cx // XS, cx % XS, lo:lo + lay.rows, :] = val[
                    cx * lay.rows:(cx + 1) * lay.rows, j * LANE:(j + 1) * LANE
                ].astype(BF)

    def rs_core(ph, pc):
        remote(s.sb[ph][pc].at[1 - c], s.cr[ph][pc], s.sems.at[ph, pc, 0], s.sems.at[ph, pc, 1], other).start()

    def rs_x(ph, pc):
        sb, cr, xs, xr = s.sb[ph][pc], s.cr[ph][pc], s.xs[ph][pc], s.xr[ph][pc]
        remote(sb.at[1 - c], cr, s.sems.at[ph, pc, 0], s.sems.at[ph, pc, 1], other).wait_recv()
        for k in x_order:
            xd = x_peer(k)
            xs[xd] = (sb[c, xd].astype(F32) + cr[xd].astype(F32)).astype(BF)
            remote(
                xs.at[xd], xr.at[x], s.sems.at[ph, pc, 2], s.sems.at[ph, pc, 3], at(c, xd, z)
            ).start()
        s.acc[pc][...] = sb[c, x].astype(F32) + cr[x].astype(F32)

    def rs_z(ph, pc):
        xr, zs, zr = s.xr[ph][pc], s.zs[ph][pc], s.zr[ph][pc]
        span = xr.at[pl.ds(0, XS - 1)]
        remote(span, span, s.sems.at[ph, pc, 2], s.sems.at[ph, pc, 3], other).wait_recv()
        total = s.acc[pc][...]
        for k in range(1, XS):
            total = total + xr[x_peer(k)].astype(F32)
        total = total.astype(BF)
        for mi in range(len(PIECES[pc])):
            chunks = nn(s.perm[...], total[mi * BR:(mi + 1) * BR])
            zs[:, mi * NS:(mi + 1) * NS, :] = chunks.reshape(Z, NS, LANE).astype(BF)

        def send(i, carry):
            zd = z_peer(z_step(i))
            remote(
                zs.at[zd], zr.at[z], s.sems.at[ph, pc, 4], s.sems.at[ph, pc, 5], at(c, x, zd)
            ).start()
            return carry

        lax.fori_loop(0, Z - 1, send, 0)

    def rs_own(ph, pc):
        zs, zr = s.zs[ph][pc], s.zr[ph][pc]
        span = zr.at[pl.ds(0, Z - 1)]
        remote(span, span, s.sems.at[ph, pc, 4], s.sems.at[ph, pc, 5], other).wait_recv()
        total = zs[z].astype(F32)
        for k in range(1, Z):
            total = total + zr[z_peer(k)].astype(F32)
        return [total[mi * NS:(mi + 1) * NS] for mi in range(len(PIECES[pc]))]

    def rs_drain(ph):
        for pc in range(len(PIECES)):
            sb, xr, zr = s.sb[ph][pc], s.xr[ph][pc], s.zr[ph][pc]
            for i, span in ((0, sb.at[1 - c]), (2, xr.at[pl.ds(0, XS - 1)]), (4, zr.at[pl.ds(0, Z - 1)])):
                remote(span, span, s.sems.at[ph, pc, i], s.sems.at[ph, pc, i + 1], other).wait_send()

    def ag_z(ph, pc, vals):
        ab, base = s.ab[ph][pc], 3 + ph
        for mi, val in enumerate(vals):
            ab[c, x, z, mi * NS:(mi + 1) * NS, :] = val.astype(BF)

        def send(i, carry):
            zd = z_peer(z_step(i))
            mine = ab.at[c, x, z]
            remote(mine, mine, s.sems.at[base, pc, 4], s.sems.at[base, pc, 5], at(c, x, zd)).start()
            return carry

        lax.fori_loop(0, Z - 1, send, 0)

    def ag_x(ph, pc):
        ab, base = s.ab[ph][pc], 3 + ph
        span = ab.at[c, x, pl.ds(0, Z - 1)]
        remote(span, span, s.sems.at[base, pc, 4], s.sems.at[base, pc, 5], other).wait_recv()
        mine = ab.at[c, x]
        for k in x_order:
            remote(
                mine, mine, s.sems.at[base, pc, 2], s.sems.at[base, pc, 3], at(c, x_peer(k), z)
            ).start()

    def ag_core(ph, pc):
        ab, base = s.ab[ph][pc], 3 + ph
        span = ab.at[c, pl.ds(0, XS - 1)]
        remote(span, span, s.sems.at[base, pc, 2], s.sems.at[base, pc, 3], other).wait_recv()
        mine = ab.at[c]
        remote(mine, mine, s.sems.at[base, pc, 0], s.sems.at[base, pc, 1], other).start()

    def unpack(ph, pc, cc, dst):
        ab = s.ab[ph][pc]

        def step(xx, carry):
            for mi, m in enumerate(PIECES[pc]):
                lay, js = layouts[m], JS[m]
                block = ab[cc, xx, :, mi * NS:(mi + 1) * NS, :].astype(F32).reshape(BR, LANE).astype(BF)
                rows = nn(s.permt[...], block).astype(BF)
                lo = pl.multiple_of((cc * XS + xx) * lay.rows, lay.rows)
                for j in range(js):
                    dst[m][pl.ds(lo, lay.rows), j * LANE:(j + 1) * LANE] = rows[j * lay.rows:(j + 1) * lay.rows]
            return carry

        lax.fori_loop(0, XS, step, 0)

    def ag_finish(ph, dst):
        for pc in range(len(PIECES)):
            unpack(ph, pc, c, dst)
        for pc in range(len(PIECES)):
            ab, base = s.ab[ph][pc], 3 + ph
            theirs = ab.at[1 - c]
            remote(theirs, theirs, s.sems.at[base, pc, 0], s.sems.at[base, pc, 1], other).wait_recv()
            unpack(ph, pc, 1 - c, dst)

    def ag_drain(ph):
        base = 3 + ph
        for pc in range(len(PIECES)):
            ab = s.ab[ph][pc]
            for i, span in ((0, ab.at[c]), (2, ab.at[c, pl.ds(0, XS - 1)]), (4, ab.at[c, x, pl.ds(0, Z - 1)])):
                remote(span, span, s.sems.at[base, pc, i], s.sems.at[base, pc, i + 1], other).wait_send()

    def colsum(val, r):
        total = jnp.broadcast_to(jnp.sum(val, axis=1, keepdims=True), (NS, LANE))
        shift = r
        while shift < NS:
            total = total + pltpu.roll(total, shift, 0)
            shift *= 2
        return total

    pieces = range(len(PIECES))

    rows_i = lax.broadcasted_iota(jnp.int32, (BR, BR), 0)
    cols_i = lax.broadcasted_iota(jnp.int32, (BR, BR), 1)
    lz, ln = log2(Z), log2(NS)
    s.perm[...] = jnp.where(
        cols_i == (((rows_i & (NS - 1)) << lz) | lax.shift_right_logical(rows_i, ln)), 1.0, 0.0
    ).astype(BF)
    s.permt[...] = jnp.where(
        rows_i == (((cols_i & (NS - 1)) << lz) | lax.shift_right_logical(cols_i, ln)), 1.0, 0.0
    ).astype(BF)
    s.pd[...] = dl.onehot()
    pft = fl.onehot_t()
    w1t, w3t, w2t = s.w1t, s.w3t, s.w2t
    w1t[...] = nt(pft, w1_ref[...]).astype(BF)
    w3t[...] = nt(pft, w3_ref[...]).astype(BF)
    w2t[...] = tn(nn(w2_ref[...], s.pd[...]).astype(BF), fl.onehot()).astype(BF)
    s.rate[...] = column(rate_ref[...])

    def scale_v(rows):
        s.vn[rows, :] = (-wide(s.rate[rows, :], DH) * v_ref[rows, :].astype(F32)).astype(BF)

    each_rows(scale_v)
    s.vp[...] = nn(s.vn[...], s.pd[...]).astype(BF)

    s.gp[...] = nt(k_ref[...], w1t[...])
    s.up[...] = nt(k_ref[...], w3t[...])

    def mix(rows):
        _, silu, _ = parts(s.gp[rows, :])
        s.mixed[rows, :] = (silu * s.up[rows, :]).astype(BF)

    each_rows(mix)
    put(0, 0, tn(s.vp[...], s.mixed[...]))
    waits = 1 + (XS - 1) + (Z - 1) + (heads - 1)
    pl.semaphore_wait(barrier, waits)
    rs_core(0, 0)
    s.db[...] = nn(s.vp[...], w2t[...])

    def backs(rows):
        _, silu, slope = parts(s.gp[rows, :])
        db = s.db[rows, :]
        s.gb[rows, :] = (db * s.up[rows, :] * slope).astype(BF)
        s.ub[rows, :] = (db * silu).astype(BF)

    each_rows(backs)
    put(0, 1, tn(s.gb[...], k_ref[...]))
    put(0, 2, tn(s.ub[...], k_ref[...]))
    rs_core(0, 1)
    for pc in pieces:
        rs_x(0, pc)
    for pc in pieces:
        rs_z(0, pc)

    priors = [None] * 3
    for m, wt in ((0, w2t), (1, w1t), (2, w3t)):
        lay, js = layouts[m], JS[m]
        lo = pl.multiple_of((c * XS + x) * lay.rows, lay.rows)
        block = jnp.concatenate(
            [wt[pl.ds(lo, lay.rows), j * LANE:(j + 1) * LANE] for j in range(js)], axis=0
        )
        s.prior[...] = nn(s.perm[...], block)
        priors[m] = s.prior[pl.ds(pl.multiple_of(z * NS, NS), NS), :]
    gain = gain_ref[...]
    high = gain.astype(BF).astype(F32)
    middle = (gain - high).astype(BF).astype(F32)
    low = gain - high - middle
    row8 = lax.broadcasted_iota(jnp.int32, (8, DH), 0)
    split = jnp.where(row8 == 0, high, jnp.where(row8 == 1, middle, jnp.where(row8 == 2, low, 0.0)))
    gain_p = jnp.sum(nn(split.astype(BF), s.pd[...]), axis=0, keepdims=True)
    s.gw[...] = nn(g_ref[...], s.pd[...]) * gain_p

    sums = [None] * 3
    moved, prior_norm, moved_norm = [None] * 3, [None] * 3, [None] * 3
    for m in range(3):
        prior_norm[m] = jnp.sqrt(colsum(priors[m] * priors[m], layouts[m].r) + EPSILON)
    for pc in pieces:
        got = rs_own(0, pc)
        fast = []
        for mi, m in enumerate(PIECES[pc]):
            moved[m] = priors[m] - got[mi]
            moved_norm[m] = jnp.sqrt(colsum(moved[m] * moved[m], layouts[m].r) + EPSILON)
            fast.append(moved[m] * (prior_norm[m] / moved_norm[m]))
        ag_z(0, pc, fast)
    for pc in pieces:
        ag_x(0, pc)
    for pc in pieces:
        ag_core(0, pc)
    f1t, f3t, f2t = s.f1t, s.f3t, s.f2t
    ag_finish(0, (f2t, f1t, f3t))

    s.qg[...] = nt(q_ref[...], f1t[...])
    s.qu[...] = nt(q_ref[...], f3t[...])

    def qmix(rows):
        _, silu, _ = parts(s.qg[rows, :])
        s.qm[rows, :] = (silu * s.qu[rows, :]).astype(BF)

    each_rows(qmix)
    s.out[...] = nt(s.qm[...], f2t[...])

    def fold(rows):
        o, w = s.out[rows, :], s.gw[rows, :]
        sq, dt = o * o, w * o
        s.sq[rows, :] = sum(sq[:, j * LANE:(j + 1) * LANE] for j in range(DH // LANE))
        s.dt[rows, :] = sum(dt[:, j * LANE:(j + 1) * LANE] for j in range(DH // LANE))

    each_rows(fold)
    row_sq = jnp.sum(s.sq[...].T, axis=0, keepdims=True)
    row_dt = jnp.sum(s.dt[...].T, axis=0, keepdims=True)
    row8t = lax.broadcasted_iota(jnp.int32, (8, T), 0)
    s.hs[...] = jnp.where(row8t == 0, row_sq, row_dt)
    for k in range(1, heads):
        remote(s.hs, s.hr.at[h], s.hsem.at[0], s.hsem.at[1], (head_peer(k), t)).start()
    span = s.hr.at[pl.ds(0, heads - 1)]
    remote(span, span, s.hsem.at[0], s.hsem.at[1], other).wait_recv()
    both = s.hs[...]
    for k in range(1, heads):
        both = both + s.hr[head_peer(k)]
    full_width = heads * DH
    square, dots = both[0:1], both[1:2]
    inverse = lax.rsqrt(square / full_width + EPSILON)
    s.inv[...] = column(inverse)
    s.coef[...] = column(inverse * inverse * inverse * dots / full_width)

    def outback(rows):
        s.ob[rows, :] = (
            wide(s.inv[rows, :], DH) * s.gw[rows, :] - s.out[rows, :] * wide(s.coef[rows, :], DH)
        ).astype(BF)

    each_rows(outback)

    put(1, 0, tn(s.ob[...], s.qm[...]))
    rs_core(1, 0)
    s.qb[...] = nn(s.ob[...], f2t[...])

    def qbacks(rows):
        _, silu, slope = parts(s.qg[rows, :])
        qb = s.qb[rows, :]
        s.qgb[rows, :] = (qb * s.qu[rows, :] * slope).astype(BF)
        s.qub[rows, :] = (qb * silu).astype(BF)

    each_rows(qbacks)
    put(1, 1, tn(s.qgb[...], q_ref[...]))
    put(1, 2, tn(s.qub[...], q_ref[...]))
    rs_core(1, 1)
    for pc in pieces:
        rs_x(1, pc)
    for pc in pieces:
        rs_z(1, pc)
    qo_ref[...] = (nn(s.qgb[...], f1t[...]) + nn(s.qub[...], f3t[...])).astype(BF)

    owned = [None] * 3
    for pc in pieces:
        got = rs_own(1, pc)
        cot = []
        for mi, m in enumerate(PIECES[pc]):
            grad, mn, pn = got[mi], moved_norm[m], prior_norm[m]
            dot = colsum(grad * moved[m], layouts[m].r)
            moved_grad = pn / mn * (grad - moved[m] * (dot / (mn * mn)))
            owned[m] = moved_grad + priors[m] * (dot / (mn * pn))
            cot.append(moved_grad)
        ag_z(1, pc, cot)
    for pc in pieces:
        ag_x(1, pc)
    for pc in pieces:
        ag_core(1, pc)
    c1t, c3t, c2t = s.c1t, s.c3t, s.c2t
    ag_finish(1, (c2t, c1t, c3t))

    s.qg[...] = nt(k_ref[...], c1t[...])
    s.qu[...] = nt(k_ref[...], c3t[...])
    s.qb[...] = nn(s.vp[...], c2t[...])

    def bars(rows):
        hidden, up, db = s.gp[rows, :], s.up[rows, :], s.db[rows, :]
        gate_bar, up_bar, mixed_bar = s.qg[rows, :], s.qu[rows, :], s.qb[rows, :]
        sg, silu, slope = parts(hidden)
        curve = sg * (1.0 - sg) * (2.0 + hidden * (1.0 - 2.0 * sg))
        s.dbb[rows, :] = (gate_bar * up * slope + up_bar * silu).astype(BF)
        s.qub[rows, :] = (gate_bar * db * slope + mixed_bar * silu).astype(BF)
        s.qgb[rows, :] = ((up_bar * db + mixed_bar * up) * slope + gate_bar * db * up * curve).astype(BF)

    each_rows(bars)
    put(2, 0, tn(s.vp[...], s.dbb[...]))
    rs_core(2, 0)
    put(2, 1, tn(s.qgb[...], k_ref[...]))
    put(2, 2, tn(s.qub[...], k_ref[...]))
    rs_core(2, 1)
    for pc in pieces:
        rs_x(2, pc)
    for pc in pieces:
        rs_z(2, pc)

    s.out[...] = nt(s.mixed[...], c2t[...]) + nt(s.dbb[...], w2t[...])

    def value(rows):
        s.vn[rows, :] = (wide(s.rate[rows, :], DH) * s.out[rows, :]).astype(BF)

    each_rows(value)
    vo_ref[...] = nt(s.vn[...], s.pd[...]).astype(BF)
    ko_ref[...] = (
        -(nn(s.gb[...], c1t[...]) + nn(s.ub[...], c3t[...]) + nn(s.qgb[...], w1t[...]) + nn(s.qub[...], w3t[...]))
    ).astype(BF)

    for pc in pieces:
        got = rs_own(2, pc)
        for mi, m in enumerate(PIECES[pc]):
            own_ref[m] = owned[m] - got[mi]
    for ph in range(3):
        rs_drain(ph)
    for ph in range(2):
        ag_drain(ph)
    hall = s.hr.at[pl.ds(0, heads - 1)]
    remote(hall, hall, s.hsem.at[0], s.hsem.at[1], other).wait_send()


class Scratch:
    def __init__(self, heads, toks, T, DH, FH):
        self.specs, self.names = [], []
        Z = toks // (CORES * XS)
        BR = DH * FH // (CORES * XS * LANE)
        NS = BR // Z

        def vm(name, *shape, dtype=BF):
            self.specs.append(pltpu.VMEM(shape, dtype))
            self.names.append(name)

        for name in ("gp", "up", "db", "qg", "qu", "qb"):
            vm(name, T, FH, dtype=F32)
        for name in ("mixed", "gb", "ub", "qm", "qgb", "qub", "dbb"):
            vm(name, T, FH)
        for name in ("vn", "vp", "ob"):
            vm(name, T, DH)
        for name in ("gw", "out"):
            vm(name, T, DH, dtype=F32)
        for name in ("rate", "inv", "coef", "sq", "dt"):
            vm(name, T, LANE, dtype=F32)
        for name in ("w1t", "w3t", "f1t", "f3t", "c1t", "c3t"):
            vm(name, FH, DH)
        for name in ("w2t", "f2t", "c2t"):
            vm(name, DH, FH)
        vm("pd", DH, DH)
        vm("perm", BR, BR)
        vm("permt", BR, BR)
        vm("prior", BR, LANE, dtype=F32)
        vm("hs", 8, T, dtype=F32)
        vm("hr", heads, 8, T, dtype=F32)
        for pc, ms in enumerate(PIECES):
            n = len(ms)
            vm(("acc", pc), n * BR, LANE, dtype=F32)
            for ph in range(3):
                vm(("sb", ph, pc), CORES, XS, n * BR, LANE)
                vm(("cr", ph, pc), XS, n * BR, LANE)
                vm(("xs", ph, pc), XS, n * BR, LANE)
                vm(("xr", ph, pc), XS, n * BR, LANE)
                vm(("zs", ph, pc), Z, n * NS, LANE)
                vm(("zr", ph, pc), Z, n * NS, LANE)
            for ph in range(2):
                vm(("ab", ph, pc), CORES, XS, Z, n * NS, LANE)
        for name, shape in (("sems", (5, len(PIECES), 6)), ("hsem", (2,))):
            self.specs.append(pltpu.SemaphoreType.DMA(shape))
            self.names.append(name)

    def bind(self, refs):
        class Refs:
            pass

        s = Refs()
        s.place = {m: (pc, mi) for pc, ms in enumerate(PIECES) for mi, m in enumerate(ms)}
        for name in ("sb", "cr", "xs", "xr", "zs", "zr"):
            setattr(s, name, [[None] * len(PIECES) for _ in range(3)])
        s.ab = [[None] * len(PIECES) for _ in range(2)]
        s.acc = [None] * len(PIECES)
        for name, ref in zip(self.names, refs):
            if isinstance(name, str):
                setattr(s, name, ref)
            elif len(name) == 2:
                s.acc[name[1]] = ref
            else:
                getattr(s, name[0])[name[1]][name[2]] = ref
        return s


def per_device(heads, toks, query, key, value, out_grad, rates, gain, w1, w3, w2):
    T, DH = query.shape
    FH = w1.shape[2]
    Z = toks // (CORES * XS)
    NS = DH * FH // (CORES * XS * LANE) // Z
    scratch = Scratch(heads, toks, T, DH, FH)

    def kernel(*refs):
        body(heads, toks, *refs[:13], scratch.bind(refs[13:]))

    vmem = pl.BlockSpec(memory_space=pltpu.VMEM)
    tokens = jax.ShapeDtypeStruct((T, DH), BF)
    qo, ko, vo, own = pl.pallas_call(
        kernel,
        out_shape=(tokens, tokens, tokens, jax.ShapeDtypeStruct((3, NS, LANE), F32)),
        in_specs=[vmem] * 9,
        out_specs=(vmem,) * 4,
        scratch_shapes=scratch.specs,
        compiler_params=pltpu.CompilerParams(
            collective_id=0, has_side_effects=True, vmem_limit_bytes=56 * 1024 * 1024
        ),
        name="lact_backward",
    )(query, key, value, out_grad, rates.reshape(1, T), gain.reshape(1, DH), w1[0], w3[0], w2[0])
    fr, dr = Layout(FH, Z).r, Layout(DH, Z).r
    down = own[0].reshape(FH // LANE, dr, LANE).transpose(0, 2, 1).reshape(CORES, XS, fr, Z, dr)
    down = down.transpose(3, 1, 0, 2, 4).reshape(1, FH, dr)
    gate = own[1].reshape(DH // LANE, fr, LANE).transpose(0, 2, 1).reshape(1, DH, fr)
    up = own[2].reshape(DH // LANE, fr, LANE).transpose(0, 2, 1).reshape(1, DH, fr)
    return qo, ko, vo, gate, up, down


def solution(mesh):
    heads, toks = mesh.shape["head"], mesh.shape["tok"]
    token_spec, weight_in, weight_out = P("tok", "head"), P("head", None, None), P("head", None, "tok")

    def step(*args):
        return per_device(heads, toks, *args)

    return jax.shard_map(
        step,
        mesh=mesh,
        in_specs=(token_spec,) * 5 + (P("head"),) + (weight_in,) * 3,
        out_specs=(token_spec,) * 3 + (weight_out,) * 3,
        check_vma=False,
    )
```

```python
import jax
import jax.numpy as jnp
from jax import lax
from jax.experimental import pallas as pl
from jax.experimental.pallas import tpu as pltpu
from jax.sharding import PartitionSpec as P

EPSILON = 1e-06
CORES = 2
XS = 4
LANE = 128
BF = jnp.bfloat16
F32 = jnp.float32
MESH = pl.DeviceIdType.MESH
VMEM_LIMIT = 56 * 1024 * 1024
PIECES = ((0,), (1,), (2,))


def nn(a, b):
    return lax.dot_general(a, b, (((1,), (0,)), ((), ())), preferred_element_type=F32)


def nt(a, b):
    return lax.dot_general(a, b, (((1,), (1,)), ((), ())), preferred_element_type=F32)


def tn(a, b):
    return lax.dot_general(a, b, (((0,), (0,)), ((), ())), preferred_element_type=F32)


def log2(n):
    return n.bit_length() - 1


class Layout:
    def __init__(self, n, zs):
        self.n, self.zs = n, zs
        self.r = n // (CORES * XS * zs)
        self.rows = self.r * zs

    def natural(self, pos):
        lz, lr, lx, lc = log2(self.zs), log2(self.r), log2(XS), log2(CORES)
        z = pos & (self.zs - 1)
        r = lax.shift_right_logical(pos, lz) & (self.r - 1)
        x = lax.shift_right_logical(pos, lz + lr) & (XS - 1)
        c = lax.shift_right_logical(pos, lz + lr + lx) & (CORES - 1)
        return (z << (lx + lc + lr)) | (x << (lc + lr)) | (c << lr) | r

    def onehot(self):
        shape = (self.n, self.n)
        rows = lax.broadcasted_iota(jnp.int32, shape, 0)
        cols = self.natural(lax.broadcasted_iota(jnp.int32, shape, 1))
        return jnp.where(rows == cols, 1.0, 0.0).astype(BF)

    def onehot_t(self):
        shape = (self.n, self.n)
        rows = self.natural(lax.broadcasted_iota(jnp.int32, shape, 0))
        cols = lax.broadcasted_iota(jnp.int32, shape, 1)
        return jnp.where(rows == cols, 1.0, 0.0).astype(BF)


INPUTS = ("w1", "w3", "k", "w2", "rate_row", "v", "g", "gain_row", "q")


def body(heads, toks, ins, outs, s):
    q_ref, k_ref, v_ref, g_ref, w1_ref, w3_ref, w2_ref = s.q, s.k, s.v, s.g, s.w1, s.w3, s.w2
    T, DH = q_ref.shape
    FH = w1_ref.shape[1]
    Z = toks // (CORES * XS)
    BR = DH * FH // (CORES * XS * LANE)
    NS = BR // Z
    fl, dl = Layout(FH, Z), Layout(DH, Z)
    layouts = (dl, fl, fl)
    JS = (FH // LANE, DH // LANE, DH // LANE)
    h = lax.axis_index("head")
    t = lax.axis_index("tok")
    c = lax.rem(t, CORES)
    x = lax.rem(t // CORES, XS)
    z = t // (CORES * XS)

    def at(c_, x_, z_):
        return (h, (z_ * XS + x_) * CORES + c_)

    other = at(1 - c, x, z)

    def x_peer(k):
        return lax.rem(x + k, XS)

    def z_peer(k):
        return lax.rem(z + k, Z)

    def head_peer(k):
        return lax.rem(h + k, heads)

    def z_step(i):
        half = (i + 1) // 2
        return Z // 2 + jnp.where(lax.rem(i, 2) == 0, half, -half)

    x_order = sorted(range(1, XS), key=lambda k: -min(k, XS - k))

    loads = {}
    for i, name in enumerate(INPUTS):
        loads[name] = pltpu.make_async_copy(ins[name], getattr(s, name), s.insem.at[i])

    barrier = pltpu.get_barrier_semaphore()
    near = [other] + [at(c, x_peer(k), z) for k in range(1, XS)]
    near += [at(c, x, z_peer(1)), at(c, x, z_peer(Z - 1))]
    near += [(head_peer(k), t) for k in range(1, heads)]
    for device in near:
        pl.semaphore_signal(barrier, inc=1, device_id=device, device_id_type=MESH)
    for name in INPUTS:
        loads[name].start()

    rounds = log2(Z) - 1

    def reach_signal(i):
        if i < rounds:
            for k in (2**i, Z - 2**i):
                pl.semaphore_signal(s.reach.at[i], inc=1, device_id=at(c, x, z_peer(k)), device_id_type=MESH)

    def reach_wait(i):
        if i < rounds:
            pl.semaphore_wait(s.reach.at[i], 2)

    RC = min(32, T)

    def each_rows(fn):
        def step(i, carry):
            fn(pl.ds(pl.multiple_of(i * RC, RC), RC))
            return carry

        lax.fori_loop(0, T // RC, step, 0)

    def remote(src, dst, send, recv, device):
        return pltpu.make_async_remote_copy(
            src_ref=src, dst_ref=dst, send_sem=send, recv_sem=recv, device_id=device, device_id_type=MESH
        )

    def wide(v, n):
        return jnp.concatenate([v] * (n // LANE), axis=1)

    def column(row):
        return jnp.broadcast_to(row, (LANE, row.shape[1])).T

    def parts(hidden):
        sg = jax.nn.sigmoid(hidden)
        return sg, hidden * sg, sg * (1.0 + hidden * (1.0 - sg))

    def put(ph, m, val):
        pc, mi = s.place[m]
        lay, js = layouts[m], JS[m]
        ref = s.sb[ph][pc]
        for cx in range(CORES * XS):
            for j in range(js):
                lo = mi * BR + j * lay.rows
                ref[cx // XS, cx % XS, lo:lo + lay.rows, :] = val[
                    cx * lay.rows:(cx + 1) * lay.rows, j * LANE:(j + 1) * LANE
                ].astype(BF)

    def rs_core(ph, pc):
        remote(s.sb[ph][pc].at[1 - c], s.cr[ph][pc], s.sems.at[ph, pc, 0], s.sems.at[ph, pc, 1], other).start()

    def rs_x(ph, pc):
        sb, cr, xs, xr = s.sb[ph][pc], s.cr[ph][pc], s.xs[ph][pc], s.xr[ph][pc]
        remote(sb.at[1 - c], cr, s.sems.at[ph, pc, 0], s.sems.at[ph, pc, 1], other).wait_recv()
        for k in x_order:
            xd = x_peer(k)
            xs[xd] = (sb[c, xd].astype(F32) + cr[xd].astype(F32)).astype(BF)
            remote(
                xs.at[xd], xr.at[x], s.sems.at[ph, pc, 2], s.sems.at[ph, pc, 3], at(c, xd, z)
            ).start()
        s.acc[pc][...] = sb[c, x].astype(F32) + cr[x].astype(F32)

    def rs_z(ph, pc):
        xr, zs, zr = s.xr[ph][pc], s.zs[ph][pc], s.zr[ph][pc]
        span = xr.at[pl.ds(0, XS - 1)]
        remote(span, span, s.sems.at[ph, pc, 2], s.sems.at[ph, pc, 3], other).wait_recv()
        total = s.acc[pc][...]
        for k in range(1, XS):
            total = total + xr[x_peer(k)].astype(F32)
        total = total.astype(BF)
        for mi in range(len(PIECES[pc])):
            chunks = nn(s.perm[...], total[mi * BR:(mi + 1) * BR])
            zs[:, mi * NS:(mi + 1) * NS, :] = chunks.reshape(Z, NS, LANE).astype(BF)

        def send(i, carry):
            zd = z_peer(z_step(i))
            remote(
                zs.at[zd], zr.at[z], s.sems.at[ph, pc, 4], s.sems.at[ph, pc, 5], at(c, x, zd)
            ).start()
            return carry

        lax.fori_loop(0, Z - 1, send, 0)

    def rs_own(ph, pc):
        zs, zr = s.zs[ph][pc], s.zr[ph][pc]
        span = zr.at[pl.ds(0, Z - 1)]
        remote(span, span, s.sems.at[ph, pc, 4], s.sems.at[ph, pc, 5], other).wait_recv()
        total = zs[z].astype(F32)
        for k in range(1, Z):
            total = total + zr[z_peer(k)].astype(F32)
        return [total[mi * NS:(mi + 1) * NS] for mi in range(len(PIECES[pc]))]

    def rs_drain(ph):
        for pc in range(len(PIECES)):
            sb, xr, zr = s.sb[ph][pc], s.xr[ph][pc], s.zr[ph][pc]
            for i, span in ((0, sb.at[1 - c]), (2, xr.at[pl.ds(0, XS - 1)]), (4, zr.at[pl.ds(0, Z - 1)])):
                remote(span, span, s.sems.at[ph, pc, i], s.sems.at[ph, pc, i + 1], other).wait_send()

    def ag_z(ph, pc, vals):
        ab, base = s.ab[ph][pc], 3 + ph
        for mi, val in enumerate(vals):
            ab[c, x, z, mi * NS:(mi + 1) * NS, :] = val.astype(BF)

        def send(i, carry):
            zd = z_peer(z_step(i))
            mine = ab.at[c, x, z]
            remote(mine, mine, s.sems.at[base, pc, 4], s.sems.at[base, pc, 5], at(c, x, zd)).start()
            return carry

        lax.fori_loop(0, Z - 1, send, 0)

    def ag_x(ph, pc):
        ab, base = s.ab[ph][pc], 3 + ph
        span = ab.at[c, x, pl.ds(0, Z - 1)]
        remote(span, span, s.sems.at[base, pc, 4], s.sems.at[base, pc, 5], other).wait_recv()
        mine = ab.at[c, x]
        for k in x_order:
            remote(
                mine, mine, s.sems.at[base, pc, 2], s.sems.at[base, pc, 3], at(c, x_peer(k), z)
            ).start()

    def ag_core(ph, pc):
        ab, base = s.ab[ph][pc], 3 + ph
        span = ab.at[c, pl.ds(0, XS - 1)]
        remote(span, span, s.sems.at[base, pc, 2], s.sems.at[base, pc, 3], other).wait_recv()
        mine = ab.at[c]
        remote(mine, mine, s.sems.at[base, pc, 0], s.sems.at[base, pc, 1], other).start()

    def unpack(ph, pc, cc, dst):
        ab = s.ab[ph][pc]
        for mi, m in enumerate(PIECES[pc]):
            lay, js = layouts[m], JS[m]
            blocks = jnp.concatenate(
                [ab[cc, xx, :, mi * NS:(mi + 1) * NS, :].astype(F32).reshape(BR, LANE) for xx in range(XS)], axis=1
            )
            rows = nn(s.permt[...], blocks.astype(BF)).astype(BF)
            for xx in range(XS):
                lo = pl.multiple_of((cc * XS + xx) * lay.rows, lay.rows)
                for j in range(js):
                    dst[m][pl.ds(lo, lay.rows), j * LANE:(j + 1) * LANE] = rows[
                        j * lay.rows:(j + 1) * lay.rows, xx * LANE:(xx + 1) * LANE
                    ]

    def ag_finish(ph, dst):
        for pc in range(len(PIECES)):
            unpack(ph, pc, c, dst)
        for pc in range(len(PIECES)):
            ab, base = s.ab[ph][pc], 3 + ph
            theirs = ab.at[1 - c]
            remote(theirs, theirs, s.sems.at[base, pc, 0], s.sems.at[base, pc, 1], other).wait_recv()
            unpack(ph, pc, 1 - c, dst)

    def ag_drain(ph):
        base = 3 + ph
        for pc in range(len(PIECES)):
            ab = s.ab[ph][pc]
            for i, span in ((0, ab.at[c]), (2, ab.at[c, pl.ds(0, XS - 1)]), (4, ab.at[c, x, pl.ds(0, Z - 1)])):
                remote(span, span, s.sems.at[base, pc, i], s.sems.at[base, pc, i + 1], other).wait_send()

    def colsum(val, r):
        total = jnp.broadcast_to(jnp.sum(val, axis=1, keepdims=True), (NS, LANE))
        shift = r
        while shift < NS:
            total = total + pltpu.roll(total, shift, 0)
            shift *= 2
        return total

    pieces = range(len(PIECES))

    rows_i = lax.broadcasted_iota(jnp.int32, (BR, BR), 0)
    cols_i = lax.broadcasted_iota(jnp.int32, (BR, BR), 1)
    lz, ln = log2(Z), log2(NS)
    s.perm[...] = jnp.where(
        cols_i == (((rows_i & (NS - 1)) << lz) | lax.shift_right_logical(rows_i, ln)), 1.0, 0.0
    ).astype(BF)
    s.permt[...] = jnp.where(
        rows_i == (((cols_i & (NS - 1)) << lz) | lax.shift_right_logical(cols_i, ln)), 1.0, 0.0
    ).astype(BF)
    pft = fl.onehot_t()
    w1t, w3t, w2t = s.w1t, s.w3t, s.w2t
    s.pd[...] = dl.onehot()
    loads["w1"].wait()
    w1t[...] = nt(pft, w1_ref[...]).astype(BF)
    loads["w3"].wait()
    w3t[...] = nt(pft, w3_ref[...]).astype(BF)

    loads["k"].wait()
    s.gp[...] = nt(k_ref[...], w1t[...])
    s.up[...] = nt(k_ref[...], w3t[...])

    def mix(rows):
        _, silu, _ = parts(s.gp[rows, :])
        s.mixed[rows, :] = (silu * s.up[rows, :]).astype(BF)

    each_rows(mix)
    loads["rate_row"].wait()
    s.rate[...] = column(s.rate_row[...])
    loads["v"].wait()

    def scale_v(rows):
        s.vn[rows, :] = (-wide(s.rate[rows, :], DH) * v_ref[rows, :].astype(F32)).astype(BF)

    each_rows(scale_v)
    s.vp[...] = nn(s.vn[...], s.pd[...]).astype(BF)
    put(0, 0, tn(s.vp[...], s.mixed[...]))
    pl.semaphore_wait(barrier, len(near))
    reach_signal(0)
    rs_core(0, 0)
    loads["w2"].wait()
    w2t[...] = tn(nn(w2_ref[...], s.pd[...]).astype(BF), fl.onehot()).astype(BF)
    s.db[...] = nn(s.vp[...], w2t[...])

    def backs(rows):
        _, silu, slope = parts(s.gp[rows, :])
        db = s.db[rows, :]
        s.gb[rows, :] = (db * s.up[rows, :] * slope).astype(BF)
        s.ub[rows, :] = (db * silu).astype(BF)

    each_rows(backs)
    put(0, 1, tn(s.gb[...], k_ref[...]))
    rs_core(0, 1)
    put(0, 2, tn(s.ub[...], k_ref[...]))
    rs_core(0, 2)
    reach_wait(0)
    reach_signal(1)
    rs_x(0, 0)
    rs_x(0, 1)
    reach_wait(1)
    reach_signal(2)
    rs_x(0, 2)
    for i in range(2, rounds):
        reach_wait(i)
        reach_signal(i + 1)
    for pc in pieces:
        rs_z(0, pc)

    priors = [None] * 3
    for m, wt in ((0, w2t), (1, w1t), (2, w3t)):
        lay, js = layouts[m], JS[m]
        lo = pl.multiple_of((c * XS + x) * lay.rows, lay.rows)
        block = jnp.concatenate(
            [wt[pl.ds(lo, lay.rows), j * LANE:(j + 1) * LANE] for j in range(js)], axis=0
        )
        s.prior[...] = nn(s.perm[...], block)
        priors[m] = s.prior[pl.ds(pl.multiple_of(z * NS, NS), NS), :]
    loads["gain_row"].wait()
    loads["g"].wait()
    loads["q"].wait()
    gain = s.gain_row[...]
    high = gain.astype(BF).astype(F32)
    middle = (gain - high).astype(BF).astype(F32)
    low = gain - high - middle
    row8 = lax.broadcasted_iota(jnp.int32, (8, DH), 0)
    split = jnp.where(row8 == 0, high, jnp.where(row8 == 1, middle, jnp.where(row8 == 2, low, 0.0)))
    gain_p = jnp.sum(nn(split.astype(BF), s.pd[...]), axis=0, keepdims=True)
    s.gw[...] = nn(g_ref[...], s.pd[...]) * gain_p

    sums = [None] * 3
    moved, prior_norm, moved_norm = [None] * 3, [None] * 3, [None] * 3
    for m in range(3):
        prior_norm[m] = jnp.sqrt(colsum(priors[m] * priors[m], layouts[m].r) + EPSILON)
    for pc in pieces:
        got = rs_own(0, pc)
        fast = []
        for mi, m in enumerate(PIECES[pc]):
            moved[m] = priors[m] - got[mi]
            moved_norm[m] = jnp.sqrt(colsum(moved[m] * moved[m], layouts[m].r) + EPSILON)
            fast.append(moved[m] * (prior_norm[m] / moved_norm[m]))
        ag_z(0, pc, fast)
    for pc in pieces:
        ag_x(0, pc)
    for pc in pieces:
        ag_core(0, pc)
    f1t, f3t, f2t = s.f1t, s.f3t, s.f2t
    ag_finish(0, (f2t, f1t, f3t))

    s.qg[...] = nt(q_ref[...], f1t[...])
    s.qu[...] = nt(q_ref[...], f3t[...])

    def qmix(rows):
        _, silu, _ = parts(s.qg[rows, :])
        s.qm[rows, :] = (silu * s.qu[rows, :]).astype(BF)

    each_rows(qmix)
    s.out[...] = nt(s.qm[...], f2t[...])

    def fold(rows):
        o, w = s.out[rows, :], s.gw[rows, :]
        sq, dt = o * o, w * o
        s.sq[rows, :] = sum(sq[:, j * LANE:(j + 1) * LANE] for j in range(DH // LANE))
        s.dt[rows, :] = sum(dt[:, j * LANE:(j + 1) * LANE] for j in range(DH // LANE))

    each_rows(fold)
    row_sq = jnp.sum(s.sq[...].T, axis=0, keepdims=True)
    row_dt = jnp.sum(s.dt[...].T, axis=0, keepdims=True)
    row8t = lax.broadcasted_iota(jnp.int32, (8, T), 0)
    s.hs[...] = jnp.where(row8t == 0, row_sq, row_dt)
    for k in range(1, heads):
        remote(s.hs, s.hr.at[h], s.hsem.at[0], s.hsem.at[1], (head_peer(k), t)).start()
    span = s.hr.at[pl.ds(0, heads - 1)]
    remote(span, span, s.hsem.at[0], s.hsem.at[1], other).wait_recv()
    both = s.hs[...]
    for k in range(1, heads):
        both = both + s.hr[head_peer(k)]
    full_width = heads * DH
    square, dots = both[0:1], both[1:2]
    inverse = lax.rsqrt(square / full_width + EPSILON)
    s.inv[...] = column(inverse)
    s.coef[...] = column(inverse * inverse * inverse * dots / full_width)

    def outback(rows):
        s.ob[rows, :] = (
            wide(s.inv[rows, :], DH) * s.gw[rows, :] - s.out[rows, :] * wide(s.coef[rows, :], DH)
        ).astype(BF)

    each_rows(outback)

    put(1, 0, tn(s.ob[...], s.qm[...]))
    rs_core(1, 0)
    s.qb[...] = nn(s.ob[...], f2t[...])

    def qbacks(rows):
        _, silu, slope = parts(s.qg[rows, :])
        qb = s.qb[rows, :]
        s.qgb[rows, :] = (qb * s.qu[rows, :] * slope).astype(BF)
        s.qub[rows, :] = (qb * silu).astype(BF)

    each_rows(qbacks)
    put(1, 1, tn(s.qgb[...], q_ref[...]))
    rs_core(1, 1)
    put(1, 2, tn(s.qub[...], q_ref[...]))
    rs_core(1, 2)
    for pc in pieces:
        rs_x(1, pc)
    for pc in pieces:
        rs_z(1, pc)
    s.qo[...] = (nn(s.qgb[...], f1t[...]) + nn(s.qub[...], f3t[...])).astype(BF)
    stores = [pltpu.make_async_copy(s.qo, outs[0], s.outsem.at[0])]
    stores[0].start()

    owned = [None] * 3
    for pc in pieces:
        got = rs_own(1, pc)
        cot = []
        for mi, m in enumerate(PIECES[pc]):
            grad, mn, pn = got[mi], moved_norm[m], prior_norm[m]
            dot = colsum(grad * moved[m], layouts[m].r)
            moved_grad = pn / mn * (grad - moved[m] * (dot / (mn * mn)))
            owned[m] = moved_grad + priors[m] * (dot / (mn * pn))
            cot.append(moved_grad)
        ag_z(1, pc, cot)
    for pc in pieces:
        ag_x(1, pc)
    for pc in pieces:
        ag_core(1, pc)
    c1t, c3t, c2t = s.c1t, s.c3t, s.c2t
    ag_finish(1, (c2t, c1t, c3t))

    s.qg[...] = nt(k_ref[...], c1t[...])
    s.qu[...] = nt(k_ref[...], c3t[...])
    s.qb[...] = nn(s.vp[...], c2t[...])

    def bars(rows):
        hidden, up, db = s.gp[rows, :], s.up[rows, :], s.db[rows, :]
        gate_bar, up_bar, mixed_bar = s.qg[rows, :], s.qu[rows, :], s.qb[rows, :]
        sg, silu, slope = parts(hidden)
        curve = sg * (1.0 - sg) * (2.0 + hidden * (1.0 - 2.0 * sg))
        s.dbb[rows, :] = (gate_bar * up * slope + up_bar * silu).astype(BF)
        s.qub[rows, :] = (gate_bar * db * slope + mixed_bar * silu).astype(BF)
        s.qgb[rows, :] = ((up_bar * db + mixed_bar * up) * slope + gate_bar * db * up * curve).astype(BF)

    each_rows(bars)
    put(2, 0, tn(s.vp[...], s.dbb[...]))
    rs_core(2, 0)
    put(2, 1, tn(s.qgb[...], k_ref[...]))
    rs_core(2, 1)
    put(2, 2, tn(s.qub[...], k_ref[...]))
    rs_core(2, 2)
    for pc in pieces:
        rs_x(2, pc)
    for pc in pieces:
        rs_z(2, pc)

    s.out[...] = nt(s.mixed[...], c2t[...]) + nt(s.dbb[...], w2t[...])

    def value(rows):
        s.vn[rows, :] = (wide(s.rate[rows, :], DH) * s.out[rows, :]).astype(BF)

    each_rows(value)
    s.vo[...] = nt(s.vn[...], s.pd[...]).astype(BF)
    stores.append(pltpu.make_async_copy(s.vo, outs[2], s.outsem.at[1]))
    stores[1].start()
    s.ko[...] = (
        -(nn(s.gb[...], c1t[...]) + nn(s.ub[...], c3t[...]) + nn(s.qgb[...], w1t[...]) + nn(s.qub[...], w3t[...]))
    ).astype(BF)
    stores.append(pltpu.make_async_copy(s.ko, outs[1], s.outsem.at[2]))
    stores[2].start()

    for pc in pieces:
        got = rs_own(2, pc)
        for mi, m in enumerate(PIECES[pc]):
            s.own[m] = owned[m] - got[mi]
    stores.append(pltpu.make_async_copy(s.own, outs[3], s.outsem.at[3]))
    stores[3].start()
    for ph in range(3):
        rs_drain(ph)
    for ph in range(2):
        ag_drain(ph)
    hall = s.hr.at[pl.ds(0, heads - 1)]
    remote(hall, hall, s.hsem.at[0], s.hsem.at[1], other).wait_send()
    for store in stores:
        store.wait()


class Scratch:
    def __init__(self, heads, toks, T, DH, FH):
        self.specs, self.names = [], []
        Z = toks // (CORES * XS)
        BR = DH * FH // (CORES * XS * LANE)
        NS = BR // Z

        def vm(name, *shape, dtype=BF):
            self.specs.append(pltpu.VMEM(shape, dtype))
            self.names.append(name)

        for name in ("gp", "up", "db", "qg", "qu", "qb"):
            vm(name, T, FH, dtype=F32)
        for name in ("mixed", "gb", "ub", "qm", "qgb", "qub", "dbb"):
            vm(name, T, FH)
        for name in ("vn", "vp", "ob"):
            vm(name, T, DH)
        for name in ("gw", "out"):
            vm(name, T, DH, dtype=F32)
        for name in ("rate", "inv", "coef", "sq", "dt"):
            vm(name, T, LANE, dtype=F32)
        for name in ("w1t", "w3t", "f1t", "f3t", "c1t", "c3t"):
            vm(name, FH, DH)
        for name in ("w2t", "f2t", "c2t"):
            vm(name, DH, FH)
        for name in ("q", "k", "v", "g", "qo", "ko", "vo"):
            vm(name, T, DH)
        vm("w1", DH, FH)
        vm("w3", DH, FH)
        vm("w2", FH, DH)
        vm("rate_row", 1, T, dtype=F32)
        vm("gain_row", 1, DH, dtype=F32)
        vm("own", 3, NS, LANE, dtype=F32)
        vm("pd", DH, DH)
        vm("perm", BR, BR)
        vm("permt", BR, BR)
        vm("prior", BR, LANE, dtype=F32)
        vm("hs", 8, T, dtype=F32)
        vm("hr", heads, 8, T, dtype=F32)
        for pc, ms in enumerate(PIECES):
            n = len(ms)
            vm(("acc", pc), n * BR, LANE, dtype=F32)
            for ph in range(3):
                vm(("sb", ph, pc), CORES, XS, n * BR, LANE)
                vm(("cr", ph, pc), XS, n * BR, LANE)
                vm(("xs", ph, pc), XS, n * BR, LANE)
                vm(("xr", ph, pc), XS, n * BR, LANE)
                vm(("zs", ph, pc), Z, n * NS, LANE)
                vm(("zr", ph, pc), Z, n * NS, LANE)
            for ph in range(2):
                vm(("ab", ph, pc), CORES, XS, Z, n * NS, LANE)
        for name, shape in (
            ("sems", (5, len(PIECES), 6)), ("hsem", (2,)), ("insem", (len(INPUTS),)), ("outsem", (4,))
        ):
            self.specs.append(pltpu.SemaphoreType.DMA(shape))
            self.names.append(name)
        self.specs.append(pltpu.SemaphoreType.REGULAR((max(1, log2(Z) - 1),)))
        self.names.append("reach")

    def bind(self, refs):
        class Refs:
            pass

        s = Refs()
        s.place = {m: (pc, mi) for pc, ms in enumerate(PIECES) for mi, m in enumerate(ms)}
        for name in ("sb", "cr", "xs", "xr", "zs", "zr"):
            setattr(s, name, [[None] * len(PIECES) for _ in range(3)])
        s.ab = [[None] * len(PIECES) for _ in range(2)]
        s.acc = [None] * len(PIECES)
        for name, ref in zip(self.names, refs):
            if isinstance(name, str):
                setattr(s, name, ref)
            elif len(name) == 2:
                s.acc[name[1]] = ref
            else:
                getattr(s, name[0])[name[1]][name[2]] = ref
        return s


def per_device(heads, toks, query, key, value, out_grad, rates, gain, w1, w3, w2):
    T, DH = query.shape
    FH = w1.shape[2]
    Z = toks // (CORES * XS)
    NS = DH * FH // (CORES * XS * LANE) // Z
    scratch = Scratch(heads, toks, T, DH, FH)

    arrays = dict(
        q=query, k=key, v=value, g=out_grad, rate_row=rates.reshape(1, T), gain_row=gain.reshape(1, DH),
        w1=w1[0], w3=w3[0], w2=w2[0],
    )

    def kernel(*refs):
        n = len(INPUTS)
        body(heads, toks, dict(zip(INPUTS, refs[:n])), refs[n:n + 4], scratch.bind(refs[n + 4:]))

    anywhere = pl.BlockSpec(memory_space=pl.ANY)
    tokens = jax.ShapeDtypeStruct((T, DH), BF)
    qo, ko, vo, own = pl.pallas_call(
        kernel,
        out_shape=(tokens, tokens, tokens, jax.ShapeDtypeStruct((3, NS, LANE), F32)),
        in_specs=[anywhere] * len(INPUTS),
        out_specs=(anywhere,) * 4,
        scratch_shapes=scratch.specs,
        compiler_params=pltpu.CompilerParams(
            collective_id=0, has_side_effects=True, vmem_limit_bytes=VMEM_LIMIT
        ),
        name="lact_backward",
    )(*(arrays[name] for name in INPUTS))
    fr, dr = Layout(FH, Z).r, Layout(DH, Z).r
    down = own[0].reshape(FH // LANE, dr, LANE).transpose(0, 2, 1).reshape(CORES, XS, fr, Z, dr)
    down = down.transpose(3, 1, 0, 2, 4).reshape(1, FH, dr)
    gate = own[1].reshape(DH // LANE, fr, LANE).transpose(0, 2, 1).reshape(1, DH, fr)
    up = own[2].reshape(DH // LANE, fr, LANE).transpose(0, 2, 1).reshape(1, DH, fr)
    return qo, ko, vo, gate, up, down


def solution(mesh):
    heads, toks = mesh.shape["head"], mesh.shape["tok"]
    token_spec, weight_in, weight_out = P("tok", "head"), P("head", None, None), P("head", None, "tok")

    def step(*args):
        return per_device(heads, toks, *args)

    return jax.shard_map(
        step,
        mesh=mesh,
        in_specs=(token_spec,) * 5 + (P("head"),) + (weight_in,) * 3,
        out_specs=(token_spec,) * 3 + (weight_out,) * 3,
        check_vma=False,
    )
```

```python
import jax
import jax.numpy as jnp
from jax import lax
from jax.experimental import pallas as pl
from jax.experimental.pallas import tpu as pltpu
from jax.sharding import PartitionSpec as P

EPSILON = 1e-06
CORES = 2
XS = 4
LANE = 128
BF = jnp.bfloat16
F32 = jnp.float32
MESH = pl.DeviceIdType.MESH
VMEM_LIMIT = 24 * 1024 * 1024
PIECES = ((0,), (1,), (2,))


def nn(a, b):
    return lax.dot_general(a, b, (((1,), (0,)), ((), ())), preferred_element_type=F32)


def nt(a, b):
    return lax.dot_general(a, b, (((1,), (1,)), ((), ())), preferred_element_type=F32)


def tn(a, b):
    return lax.dot_general(a, b, (((0,), (0,)), ((), ())), preferred_element_type=F32)


def log2(n):
    return n.bit_length() - 1


class Layout:
    def __init__(self, n, zs):
        self.n, self.zs = n, zs
        self.r = n // (CORES * XS * zs)
        self.rows = self.r * zs

    def natural(self, pos):
        lz, lr, lx, lc = log2(self.zs), log2(self.r), log2(XS), log2(CORES)
        z = pos & (self.zs - 1)
        r = lax.shift_right_logical(pos, lz) & (self.r - 1)
        x = lax.shift_right_logical(pos, lz + lr) & (XS - 1)
        c = lax.shift_right_logical(pos, lz + lr + lx) & (CORES - 1)
        return (z << (lx + lc + lr)) | (x << (lc + lr)) | (c << lr) | r

    def onehot(self):
        shape = (self.n, self.n)
        rows = lax.broadcasted_iota(jnp.int32, shape, 0)
        cols = self.natural(lax.broadcasted_iota(jnp.int32, shape, 1))
        return jnp.where(rows == cols, 1.0, 0.0).astype(BF)

    def onehot_t(self):
        shape = (self.n, self.n)
        rows = self.natural(lax.broadcasted_iota(jnp.int32, shape, 0))
        cols = lax.broadcasted_iota(jnp.int32, shape, 1)
        return jnp.where(rows == cols, 1.0, 0.0).astype(BF)


INPUTS = ("w1", "w3", "k", "w2", "rate_row", "v", "g", "gain_row", "q")


def body(heads, toks, ins, outs, s):
    q_ref, k_ref, v_ref, g_ref, w1_ref, w3_ref, w2_ref = s.q, s.k, s.v, s.g, s.w1, s.w3, s.w2
    T, DH = q_ref.shape
    FH = w1_ref.shape[1]
    Z = toks // (CORES * XS)
    BR = DH * FH // (CORES * XS * LANE)
    NS = BR // Z
    fl, dl = Layout(FH, Z), Layout(DH, Z)
    layouts = (dl, fl, fl)
    JS = (FH // LANE, DH // LANE, DH // LANE)
    h = lax.axis_index("head")
    t = lax.axis_index("tok")
    c = lax.rem(t, CORES)
    x = lax.rem(t // CORES, XS)
    z = t // (CORES * XS)

    def at(c_, x_, z_):
        return (h, (z_ * XS + x_) * CORES + c_)

    other = at(1 - c, x, z)

    def x_peer(k):
        return lax.rem(x + k, XS)

    def z_peer(k):
        return lax.rem(z + k, Z)

    def head_peer(k):
        return lax.rem(h + k, heads)

    def z_step(i):
        half = (i + 1) // 2
        return Z // 2 + jnp.where(lax.rem(i, 2) == 0, half, -half)

    x_order = sorted(range(1, XS), key=lambda k: -min(k, XS - k))

    loads = {}
    for i, name in enumerate(INPUTS):
        loads[name] = pltpu.make_async_copy(ins[name], getattr(s, name), s.insem.at[i])

    barrier = pltpu.get_barrier_semaphore()
    near = [other] + [at(c, x_peer(k), z) for k in range(1, XS)]
    near += [at(c, x, z_peer(1)), at(c, x, z_peer(Z - 1))]
    near += [(head_peer(k), t) for k in range(1, heads)]
    for device in near:
        pl.semaphore_signal(barrier, inc=1, device_id=device, device_id_type=MESH)
    for name in INPUTS:
        loads[name].start()

    rounds = log2(Z) - 1

    def reach_signal(i):
        if i < rounds:
            for k in (2**i, Z - 2**i):
                pl.semaphore_signal(s.reach.at[i], inc=1, device_id=at(c, x, z_peer(k)), device_id_type=MESH)

    def reach_wait(i):
        if i < rounds:
            pl.semaphore_wait(s.reach.at[i], 2)

    RC = min(32, T)

    def each_rows(fn):
        def step(i, carry):
            fn(pl.ds(pl.multiple_of(i * RC, RC), RC))
            return carry

        lax.fori_loop(0, T // RC, step, 0)

    def remote(src, dst, send, recv, device):
        return pltpu.make_async_remote_copy(
            src_ref=src, dst_ref=dst, send_sem=send, recv_sem=recv, device_id=device, device_id_type=MESH
        )

    def wide(v, n):
        return jnp.concatenate([v] * (n // LANE), axis=1)

    def column(row):
        return jnp.broadcast_to(row, (LANE, row.shape[1])).T

    def parts(hidden):
        sg = jax.nn.sigmoid(hidden)
        return sg, hidden * sg, sg * (1.0 + hidden * (1.0 - sg))

    def put(ph, m, val):
        pc, mi = s.place[m]
        lay, js = layouts[m], JS[m]
        ref = s.sb[ph][pc]
        for cx in range(CORES * XS):
            for j in range(js):
                lo = mi * BR + j * lay.rows
                ref[cx // XS, cx % XS, lo:lo + lay.rows, :] = val[
                    cx * lay.rows:(cx + 1) * lay.rows, j * LANE:(j + 1) * LANE
                ].astype(BF)

    def rs_core(ph, pc):
        remote(s.sb[ph][pc].at[1 - c], s.cr[ph][pc], s.sems.at[ph, pc, 0], s.sems.at[ph, pc, 1], other).start()

    def rs_x(ph, pc):
        sb, cr, xs, xr = s.sb[ph][pc], s.cr[ph][pc], s.xs[ph][pc], s.xr[ph][pc]
        remote(sb.at[1 - c], cr, s.sems.at[ph, pc, 0], s.sems.at[ph, pc, 1], other).wait_recv()
        for k in x_order:
            xd = x_peer(k)
            xs[xd] = (sb[c, xd].astype(F32) + cr[xd].astype(F32)).astype(BF)
            remote(
                xs.at[xd], xr.at[x], s.sems.at[ph, pc, 2], s.sems.at[ph, pc, 3], at(c, xd, z)
            ).start()
        s.acc[pc][...] = sb[c, x].astype(F32) + cr[x].astype(F32)

    def rs_z(ph, pc):
        xr, zs, zr = s.xr[ph][pc], s.zs[ph][pc], s.zr[ph][pc]
        span = xr.at[pl.ds(0, XS - 1)]
        remote(span, span, s.sems.at[ph, pc, 2], s.sems.at[ph, pc, 3], other).wait_recv()
        total = s.acc[pc][...]
        for k in range(1, XS):
            total = total + xr[x_peer(k)].astype(F32)
        total = total.astype(BF)
        for mi in range(len(PIECES[pc])):
            chunks = nn(s.perm[...], total[mi * BR:(mi + 1) * BR])
            zs[:, mi * NS:(mi + 1) * NS, :] = chunks.reshape(Z, NS, LANE).astype(BF)

        def send(i, carry):
            zd = z_peer(z_step(i))
            remote(
                zs.at[zd], zr.at[z], s.sems.at[ph, pc, 4], s.sems.at[ph, pc, 5], at(c, x, zd)
            ).start()
            return carry

        lax.fori_loop(0, Z - 1, send, 0)

    def rs_own(ph, pc):
        zs, zr = s.zs[ph][pc], s.zr[ph][pc]
        span = zr.at[pl.ds(0, Z - 1)]
        remote(span, span, s.sems.at[ph, pc, 4], s.sems.at[ph, pc, 5], other).wait_recv()
        total = zs[z].astype(F32)
        for k in range(1, Z):
            total = total + zr[z_peer(k)].astype(F32)
        return [total[mi * NS:(mi + 1) * NS] for mi in range(len(PIECES[pc]))]

    def rs_drain(ph):
        for pc in range(len(PIECES)):
            sb, xr, zr = s.sb[ph][pc], s.xr[ph][pc], s.zr[ph][pc]
            for i, span in ((0, sb.at[1 - c]), (2, xr.at[pl.ds(0, XS - 1)]), (4, zr.at[pl.ds(0, Z - 1)])):
                remote(span, span, s.sems.at[ph, pc, i], s.sems.at[ph, pc, i + 1], other).wait_send()

    def ag_z(ph, pc, vals):
        ab, base = s.ab[ph][pc], 3 + ph
        for mi, val in enumerate(vals):
            ab[c, x, z, mi * NS:(mi + 1) * NS, :] = val.astype(BF)

        def send(i, carry):
            zd = z_peer(z_step(i))
            mine = ab.at[c, x, z]
            remote(mine, mine, s.sems.at[base, pc, 4], s.sems.at[base, pc, 5], at(c, x, zd)).start()
            return carry

        lax.fori_loop(0, Z - 1, send, 0)

    def ag_x(ph, pc):
        ab, base = s.ab[ph][pc], 3 + ph
        span = ab.at[c, x, pl.ds(0, Z - 1)]
        remote(span, span, s.sems.at[base, pc, 4], s.sems.at[base, pc, 5], other).wait_recv()
        mine = ab.at[c, x]
        for k in x_order:
            remote(
                mine, mine, s.sems.at[base, pc, 2], s.sems.at[base, pc, 3], at(c, x_peer(k), z)
            ).start()

    def ag_core(ph, pc):
        ab, base = s.ab[ph][pc], 3 + ph
        span = ab.at[c, pl.ds(0, XS - 1)]
        remote(span, span, s.sems.at[base, pc, 2], s.sems.at[base, pc, 3], other).wait_recv()
        mine = ab.at[c]
        remote(mine, mine, s.sems.at[base, pc, 0], s.sems.at[base, pc, 1], other).start()

    def unpack(ph, pc, cc, dst):
        ab = s.ab[ph][pc]
        for mi, m in enumerate(PIECES[pc]):
            lay, js = layouts[m], JS[m]
            blocks = jnp.concatenate(
                [ab[cc, xx, :, mi * NS:(mi + 1) * NS, :].astype(F32).reshape(BR, LANE) for xx in range(XS)], axis=1
            )
            rows = nn(s.permt[...], blocks.astype(BF)).astype(BF)
            for xx in range(XS):
                lo = pl.multiple_of((cc * XS + xx) * lay.rows, lay.rows)
                for j in range(js):
                    dst[m][pl.ds(lo, lay.rows), j * LANE:(j + 1) * LANE] = rows[
                        j * lay.rows:(j + 1) * lay.rows, xx * LANE:(xx + 1) * LANE
                    ]

    def ag_finish(ph, dst):
        for pc in range(len(PIECES)):
            unpack(ph, pc, c, dst)
        for pc in range(len(PIECES)):
            ab, base = s.ab[ph][pc], 3 + ph
            theirs = ab.at[1 - c]
            remote(theirs, theirs, s.sems.at[base, pc, 0], s.sems.at[base, pc, 1], other).wait_recv()
            unpack(ph, pc, 1 - c, dst)

    def ag_drain(ph):
        base = 3 + ph
        for pc in range(len(PIECES)):
            ab = s.ab[ph][pc]
            for i, span in ((0, ab.at[c]), (2, ab.at[c, pl.ds(0, XS - 1)]), (4, ab.at[c, x, pl.ds(0, Z - 1)])):
                remote(span, span, s.sems.at[base, pc, i], s.sems.at[base, pc, i + 1], other).wait_send()

    def colsum(val, r):
        total = jnp.broadcast_to(jnp.sum(val, axis=1, keepdims=True), (NS, LANE))
        shift = r
        while shift < NS:
            total = total + pltpu.roll(total, shift, 0)
            shift *= 2
        return total

    pieces = range(len(PIECES))

    def put_down(val):
        high = val.astype(BF).astype(F32)
        middle = (val - high).astype(BF).astype(F32)
        low = val - high - middle
        split = jnp.concatenate([high, middle, low, jnp.zeros_like(low)], axis=0).astype(BF)
        total = None
        for j in range(JS[0]):
            part = nn(split, s.pft[j * LANE:(j + 1) * LANE, :])
            part = part[0:NS] + part[NS:2 * NS] + part[2 * NS:3 * NS]
            part = part[j * dl.r:(j + 1) * dl.r]
            total = part if total is None else total + part
        s.own0[...] = total

    rows_i = lax.broadcasted_iota(jnp.int32, (BR, BR), 0)
    cols_i = lax.broadcasted_iota(jnp.int32, (BR, BR), 1)
    lz, ln = log2(Z), log2(NS)
    s.perm[...] = jnp.where(
        cols_i == (((rows_i & (NS - 1)) << lz) | lax.shift_right_logical(rows_i, ln)), 1.0, 0.0
    ).astype(BF)
    s.permt[...] = jnp.where(
        rows_i == (((cols_i & (NS - 1)) << lz) | lax.shift_right_logical(cols_i, ln)), 1.0, 0.0
    ).astype(BF)
    s.pft[...] = fl.onehot_t()
    w1t, w3t, w2t = s.w1t, s.w3t, s.w2t
    s.pd[...] = dl.onehot()
    loads["w1"].wait()
    w1t[...] = nt(s.pft[...], w1_ref[...]).astype(BF)
    loads["w3"].wait()
    w3t[...] = nt(s.pft[...], w3_ref[...]).astype(BF)

    loads["k"].wait()
    s.gp[...] = nt(k_ref[...], w1t[...])
    s.up[...] = nt(k_ref[...], w3t[...])

    def mix(rows):
        _, silu, _ = parts(s.gp[rows, :])
        s.mixed[rows, :] = (silu * s.up[rows, :]).astype(BF)

    each_rows(mix)
    loads["rate_row"].wait()
    s.rate[...] = column(s.rate_row[...])
    loads["v"].wait()

    def scale_v(rows):
        s.vn[rows, :] = (-wide(s.rate[rows, :], DH) * v_ref[rows, :].astype(F32)).astype(BF)

    each_rows(scale_v)
    s.vp[...] = nn(s.vn[...], s.pd[...]).astype(BF)
    put(0, 0, tn(s.vp[...], s.mixed[...]))
    pl.semaphore_wait(barrier, len(near))
    reach_signal(0)
    rs_core(0, 0)
    loads["w2"].wait()
    w2t[...] = tn(nn(w2_ref[...], s.pd[...]).astype(BF), fl.onehot()).astype(BF)
    s.db[...] = nn(s.vp[...], w2t[...])

    def backs(rows):
        _, silu, slope = parts(s.gp[rows, :])
        db = s.db[rows, :]
        s.gb[rows, :] = (db * s.up[rows, :] * slope).astype(BF)
        s.ub[rows, :] = (db * silu).astype(BF)

    each_rows(backs)
    put(0, 1, tn(s.gb[...], k_ref[...]))
    rs_core(0, 1)
    put(0, 2, tn(s.ub[...], k_ref[...]))
    rs_core(0, 2)
    reach_wait(0)
    reach_signal(1)
    rs_x(0, 0)
    rs_x(0, 1)
    reach_wait(1)
    reach_signal(2)
    rs_x(0, 2)
    for i in range(2, rounds):
        reach_wait(i)
        reach_signal(i + 1)
    for pc in pieces:
        rs_z(0, pc)

    priors = [None] * 3
    for m, wt in ((0, w2t), (1, w1t), (2, w3t)):
        lay, js = layouts[m], JS[m]
        lo = pl.multiple_of((c * XS + x) * lay.rows, lay.rows)
        block = jnp.concatenate(
            [wt[pl.ds(lo, lay.rows), j * LANE:(j + 1) * LANE] for j in range(js)], axis=0
        )
        s.prior[...] = nn(s.perm[...], block)
        priors[m] = s.prior[pl.ds(pl.multiple_of(z * NS, NS), NS), :]
    loads["gain_row"].wait()
    loads["g"].wait()
    loads["q"].wait()
    gain = s.gain_row[...]
    high = gain.astype(BF).astype(F32)
    middle = (gain - high).astype(BF).astype(F32)
    low = gain - high - middle
    row8 = lax.broadcasted_iota(jnp.int32, (8, DH), 0)
    split = jnp.where(row8 == 0, high, jnp.where(row8 == 1, middle, jnp.where(row8 == 2, low, 0.0)))
    gain_p = jnp.sum(nn(split.astype(BF), s.pd[...]), axis=0, keepdims=True)
    s.gw[...] = nn(g_ref[...], s.pd[...]) * gain_p

    sums = [None] * 3
    moved, prior_norm, moved_norm = [None] * 3, [None] * 3, [None] * 3
    for m in range(3):
        prior_norm[m] = jnp.sqrt(colsum(priors[m] * priors[m], layouts[m].r) + EPSILON)
    for pc in pieces:
        got = rs_own(0, pc)
        fast = []
        for mi, m in enumerate(PIECES[pc]):
            moved[m] = priors[m] - got[mi]
            moved_norm[m] = jnp.sqrt(colsum(moved[m] * moved[m], layouts[m].r) + EPSILON)
            fast.append(moved[m] * (prior_norm[m] / moved_norm[m]))
        ag_z(0, pc, fast)
    for pc in pieces:
        ag_x(0, pc)
    for pc in pieces:
        ag_core(0, pc)
    f1t, f3t, f2t = s.f1t, s.f3t, s.f2t
    ag_finish(0, (f2t, f1t, f3t))

    s.qg[...] = nt(q_ref[...], f1t[...])
    s.qu[...] = nt(q_ref[...], f3t[...])

    def qmix(rows):
        _, silu, _ = parts(s.qg[rows, :])
        s.qm[rows, :] = (silu * s.qu[rows, :]).astype(BF)

    each_rows(qmix)
    s.out[...] = nt(s.qm[...], f2t[...])

    def fold(rows):
        o, w = s.out[rows, :], s.gw[rows, :]
        sq, dt = o * o, w * o
        s.sq[rows, :] = sum(sq[:, j * LANE:(j + 1) * LANE] for j in range(DH // LANE))
        s.dt[rows, :] = sum(dt[:, j * LANE:(j + 1) * LANE] for j in range(DH // LANE))

    each_rows(fold)
    row_sq = jnp.sum(s.sq[...].T, axis=0, keepdims=True)
    row_dt = jnp.sum(s.dt[...].T, axis=0, keepdims=True)
    row8t = lax.broadcasted_iota(jnp.int32, (8, T), 0)
    s.hs[...] = jnp.where(row8t == 0, row_sq, row_dt)
    for k in range(1, heads):
        remote(s.hs, s.hr.at[h], s.hsem.at[0], s.hsem.at[1], (head_peer(k), t)).start()
    span = s.hr.at[pl.ds(0, heads - 1)]
    remote(span, span, s.hsem.at[0], s.hsem.at[1], other).wait_recv()
    both = s.hs[...]
    for k in range(1, heads):
        both = both + s.hr[head_peer(k)]
    full_width = heads * DH
    square, dots = both[0:1], both[1:2]
    inverse = lax.rsqrt(square / full_width + EPSILON)
    s.inv[...] = column(inverse)
    s.coef[...] = column(inverse * inverse * inverse * dots / full_width)

    def outback(rows):
        s.ob[rows, :] = (
            wide(s.inv[rows, :], DH) * s.gw[rows, :] - s.out[rows, :] * wide(s.coef[rows, :], DH)
        ).astype(BF)

    each_rows(outback)

    put(1, 0, tn(s.ob[...], s.qm[...]))
    rs_core(1, 0)
    s.qb[...] = nn(s.ob[...], f2t[...])

    def qbacks(rows):
        _, silu, slope = parts(s.qg[rows, :])
        qb = s.qb[rows, :]
        s.qgb[rows, :] = (qb * s.qu[rows, :] * slope).astype(BF)
        s.qub[rows, :] = (qb * silu).astype(BF)

    each_rows(qbacks)
    put(1, 1, tn(s.qgb[...], q_ref[...]))
    rs_core(1, 1)
    put(1, 2, tn(s.qub[...], q_ref[...]))
    rs_core(1, 2)
    for pc in pieces:
        rs_x(1, pc)
    for pc in pieces:
        rs_z(1, pc)
    s.qo[...] = (nn(s.qgb[...], f1t[...]) + nn(s.qub[...], f3t[...])).astype(BF)
    stores = [pltpu.make_async_copy(s.qo, outs[0], s.outsem.at[0])]
    stores[0].start()

    owned = [None] * 3
    for pc in pieces:
        got = rs_own(1, pc)
        cot = []
        for mi, m in enumerate(PIECES[pc]):
            grad, mn, pn = got[mi], moved_norm[m], prior_norm[m]
            dot = colsum(grad * moved[m], layouts[m].r)
            moved_grad = pn / mn * (grad - moved[m] * (dot / (mn * mn)))
            owned[m] = moved_grad + priors[m] * (dot / (mn * pn))
            cot.append(moved_grad)
        ag_z(1, pc, cot)
    for pc in pieces:
        ag_x(1, pc)
    for pc in pieces:
        ag_core(1, pc)
    c1t, c3t, c2t = s.c1t, s.c3t, s.c2t
    ag_finish(1, (c2t, c1t, c3t))

    s.qg[...] = nt(k_ref[...], c1t[...])
    s.qu[...] = nt(k_ref[...], c3t[...])
    s.qb[...] = nn(s.vp[...], c2t[...])

    def bars(rows):
        hidden, up, db = s.gp[rows, :], s.up[rows, :], s.db[rows, :]
        gate_bar, up_bar, mixed_bar = s.qg[rows, :], s.qu[rows, :], s.qb[rows, :]
        sg, silu, slope = parts(hidden)
        curve = sg * (1.0 - sg) * (2.0 + hidden * (1.0 - 2.0 * sg))
        s.dbb[rows, :] = (gate_bar * up * slope + up_bar * silu).astype(BF)
        s.qub[rows, :] = (gate_bar * db * slope + mixed_bar * silu).astype(BF)
        s.qgb[rows, :] = ((up_bar * db + mixed_bar * up) * slope + gate_bar * db * up * curve).astype(BF)

    each_rows(bars)
    put(2, 0, tn(s.vp[...], s.dbb[...]))
    rs_core(2, 0)
    put(2, 1, tn(s.qgb[...], k_ref[...]))
    rs_core(2, 1)
    put(2, 2, tn(s.qub[...], k_ref[...]))
    rs_core(2, 2)
    for pc in pieces:
        rs_x(2, pc)
    for pc in pieces:
        rs_z(2, pc)

    s.out[...] = nt(s.mixed[...], c2t[...]) + nt(s.dbb[...], w2t[...])

    def value(rows):
        s.vn[rows, :] = (wide(s.rate[rows, :], DH) * s.out[rows, :]).astype(BF)

    each_rows(value)
    s.vo[...] = nt(s.vn[...], s.pd[...]).astype(BF)
    stores.append(pltpu.make_async_copy(s.vo, outs[2], s.outsem.at[1]))
    stores[1].start()
    s.ko[...] = (
        -(nn(s.gb[...], c1t[...]) + nn(s.ub[...], c3t[...]) + nn(s.qgb[...], w1t[...]) + nn(s.qub[...], w3t[...]))
    ).astype(BF)
    stores.append(pltpu.make_async_copy(s.ko, outs[1], s.outsem.at[2]))
    stores[2].start()

    for pc in pieces:
        got = rs_own(2, pc)
        for mi, m in enumerate(PIECES[pc]):
            final = owned[m] - got[mi]
            if m == 0:
                put_down(final)
                stores.append(pltpu.make_async_copy(s.own0, outs[3], s.outsem.at[3]))
            else:
                own = (s.own1, s.own2)[m - 1]
                own[...] = final
                stores.append(pltpu.make_async_copy(own, outs[3 + m], s.outsem.at[3 + m]))
            stores[-1].start()
    for ph in range(3):
        rs_drain(ph)
    for ph in range(2):
        ag_drain(ph)
    hall = s.hr.at[pl.ds(0, heads - 1)]
    remote(hall, hall, s.hsem.at[0], s.hsem.at[1], other).wait_send()
    for store in stores:
        store.wait()


class Scratch:
    def __init__(self, heads, toks, T, DH, FH):
        self.specs, self.names = [], []
        Z = toks // (CORES * XS)
        BR = DH * FH // (CORES * XS * LANE)
        NS = BR // Z

        def vm(name, *shape, dtype=BF):
            self.specs.append(pltpu.VMEM(shape, dtype))
            self.names.append(name)

        for name in ("gp", "up", "db", "qg", "qu", "qb"):
            vm(name, T, FH, dtype=F32)
        for name in ("mixed", "gb", "ub", "qm", "qgb", "qub", "dbb"):
            vm(name, T, FH)
        for name in ("vn", "vp", "ob"):
            vm(name, T, DH)
        for name in ("gw", "out"):
            vm(name, T, DH, dtype=F32)
        for name in ("rate", "inv", "coef", "sq", "dt"):
            vm(name, T, LANE, dtype=F32)
        for name in ("w1t", "w3t", "f1t", "f3t", "c1t", "c3t"):
            vm(name, FH, DH)
        for name in ("w2t", "f2t", "c2t"):
            vm(name, DH, FH)
        for name in ("q", "k", "v", "g", "qo", "ko", "vo"):
            vm(name, T, DH)
        vm("w1", DH, FH)
        vm("w3", DH, FH)
        vm("w2", FH, DH)
        vm("rate_row", 1, T, dtype=F32)
        vm("gain_row", 1, DH, dtype=F32)
        vm("own0", Layout(DH, Z).r, FH, dtype=F32)
        vm("own1", NS, LANE, dtype=F32)
        vm("own2", NS, LANE, dtype=F32)
        vm("pft", FH, FH)
        vm("pd", DH, DH)
        vm("perm", BR, BR)
        vm("permt", BR, BR)
        vm("prior", BR, LANE, dtype=F32)
        vm("hs", 8, T, dtype=F32)
        vm("hr", heads, 8, T, dtype=F32)
        for pc, ms in enumerate(PIECES):
            n = len(ms)
            vm(("acc", pc), n * BR, LANE, dtype=F32)
            for ph in range(3):
                vm(("sb", ph, pc), CORES, XS, n * BR, LANE)
                vm(("cr", ph, pc), XS, n * BR, LANE)
                vm(("xs", ph, pc), XS, n * BR, LANE)
                vm(("xr", ph, pc), XS, n * BR, LANE)
                vm(("zs", ph, pc), Z, n * NS, LANE)
                vm(("zr", ph, pc), Z, n * NS, LANE)
            for ph in range(2):
                vm(("ab", ph, pc), CORES, XS, Z, n * NS, LANE)
        for name, shape in (
            ("sems", (5, len(PIECES), 6)), ("hsem", (2,)), ("insem", (len(INPUTS),)), ("outsem", (6,))
        ):
            self.specs.append(pltpu.SemaphoreType.DMA(shape))
            self.names.append(name)
        self.specs.append(pltpu.SemaphoreType.REGULAR((max(1, log2(Z) - 1),)))
        self.names.append("reach")

    def bind(self, refs):
        class Refs:
            pass

        s = Refs()
        s.place = {m: (pc, mi) for pc, ms in enumerate(PIECES) for mi, m in enumerate(ms)}
        for name in ("sb", "cr", "xs", "xr", "zs", "zr"):
            setattr(s, name, [[None] * len(PIECES) for _ in range(3)])
        s.ab = [[None] * len(PIECES) for _ in range(2)]
        s.acc = [None] * len(PIECES)
        for name, ref in zip(self.names, refs):
            if isinstance(name, str):
                setattr(s, name, ref)
            elif len(name) == 2:
                s.acc[name[1]] = ref
            else:
                getattr(s, name[0])[name[1]][name[2]] = ref
        return s


def per_device(heads, toks, query, key, value, out_grad, rates, gain, w1, w3, w2):
    T, DH = query.shape
    FH = w1.shape[2]
    Z = toks // (CORES * XS)
    NS = DH * FH // (CORES * XS * LANE) // Z
    scratch = Scratch(heads, toks, T, DH, FH)

    arrays = dict(
        q=query, k=key, v=value, g=out_grad, rate_row=rates.reshape(1, T), gain_row=gain.reshape(1, DH),
        w1=w1[0], w3=w3[0], w2=w2[0],
    )

    def kernel(*refs):
        n = len(INPUTS)
        body(heads, toks, dict(zip(INPUTS, refs[:n])), refs[n:n + 6], scratch.bind(refs[n + 6:]))

    anywhere, hbm = pl.BlockSpec(memory_space=pl.ANY), pl.BlockSpec(memory_space=pltpu.HBM)
    tokens = jax.ShapeDtypeStruct((T, DH), BF)
    fr, dr = Layout(FH, Z).r, Layout(DH, Z).r
    columns = jax.ShapeDtypeStruct((NS, LANE), F32)
    shapes = (tokens, tokens, tokens, jax.ShapeDtypeStruct((dr, FH), F32), columns, columns)
    results = pl.pallas_call(
        kernel,
        out_shape=shapes,
        in_specs=[hbm] * len(INPUTS),
        out_specs=(anywhere,) * 6,
        scratch_shapes=scratch.specs,
        compiler_params=pltpu.CompilerParams(
            collective_id=0, has_side_effects=True, vmem_limit_bytes=VMEM_LIMIT
        ),
        name="lact_backward",
    )(*(pltpu.with_memory_space_constraint(arrays[name], pltpu.HBM) for name in INPUTS))

    def hand_on(*refs):
        sems = refs[12]
        copies = [pltpu.make_async_copy(refs[i], refs[6 + i], sems.at[i]) for i in range(6)]
        for copy in copies:
            copy.start()
        for copy in copies:
            copy.wait()

    qo, ko, vo, down, gate, up = pl.pallas_call(
        hand_on,
        out_shape=shapes,
        in_specs=[anywhere] * 6,
        out_specs=(hbm,) * 6,
        scratch_shapes=[pltpu.SemaphoreType.DMA((6,))],
        compiler_params=pltpu.CompilerParams(vmem_limit_bytes=1024 * 1024),
        name="hand_on",
    )(*results)
    down = down.T.reshape(1, FH, dr)
    gate = gate.reshape(DH // LANE, fr, LANE).transpose(0, 2, 1).reshape(1, DH, fr)
    up = up.reshape(DH // LANE, fr, LANE).transpose(0, 2, 1).reshape(1, DH, fr)
    return qo, ko, vo, gate, up, down


def solution(mesh):
    heads, toks = mesh.shape["head"], mesh.shape["tok"]
    token_spec, weight_in, weight_out = P("tok", "head"), P("head", None, None), P("head", None, "tok")

    def step(*args):
        return per_device(heads, toks, *args)

    return jax.shard_map(
        step,
        mesh=mesh,
        in_specs=(token_spec,) * 5 + (P("head"),) + (weight_in,) * 3,
        out_specs=(token_spec,) * 3 + (weight_out,) * 3,
        check_vma=False,
    )
```

```python
import jax
import jax.numpy as jnp
from jax import lax
from jax.experimental import pallas as pl
from jax.experimental.pallas import tpu as pltpu
from jax.sharding import PartitionSpec as P

EPSILON = 1e-06
CORES = 2
XS = 4
LANE = 128
BF = jnp.bfloat16
F32 = jnp.float32
MESH = pl.DeviceIdType.MESH
VMEM_LIMIT = 24 * 1024 * 1024
QUADS = 4
MATS = 3


def nn(a, b):
    return lax.dot_general(a, b, (((1,), (0,)), ((), ())), preferred_element_type=F32)


def nt(a, b):
    return lax.dot_general(a, b, (((1,), (1,)), ((), ())), preferred_element_type=F32)


def tn(a, b):
    return lax.dot_general(a, b, (((0,), (0,)), ((), ())), preferred_element_type=F32)


def log2(n):
    return n.bit_length() - 1


class Layout:
    def __init__(self, n, zs):
        self.n, self.zs = n, zs
        self.r = n // (CORES * XS * zs)
        self.rows = self.r * zs
        self.quad = self.rows // QUADS

    def natural(self, pos):
        lq, ll, lr, lx, lc = log2(QUADS), log2(self.zs // QUADS), log2(self.r), log2(XS), log2(CORES)
        low = pos & (self.zs // QUADS - 1)
        r = lax.shift_right_logical(pos, ll) & (self.r - 1)
        q = lax.shift_right_logical(pos, ll + lr) & (QUADS - 1)
        x = lax.shift_right_logical(pos, ll + lr + lq) & (XS - 1)
        c = lax.shift_right_logical(pos, ll + lr + lq + lx) & (CORES - 1)
        z = (q << ll) | low
        return (z << (lx + lc + lr)) | (x << (lc + lr)) | (c << lr) | r

    def chunk_row(self, row, per_owner):
        lq, ll, lr = log2(QUADS), log2(self.zs // QUADS), log2(self.r)
        low = row & (self.zs // QUADS - 1)
        r = lax.shift_right_logical(row, ll) & (self.r - 1)
        q = lax.shift_right_logical(row, ll + lr) & (QUADS - 1)
        j = lax.shift_right_logical(row, ll + lr + lq)
        return (((q << ll) | low) << log2(per_owner)) | (j << lr) | r

    def onehot(self):
        shape = (self.n, self.n)
        rows = lax.broadcasted_iota(jnp.int32, shape, 0)
        cols = self.natural(lax.broadcasted_iota(jnp.int32, shape, 1))
        return jnp.where(rows == cols, 1.0, 0.0).astype(BF)

    def onehot_t(self):
        shape = (self.n, self.n)
        rows = self.natural(lax.broadcasted_iota(jnp.int32, shape, 0))
        cols = lax.broadcasted_iota(jnp.int32, shape, 1)
        return jnp.where(rows == cols, 1.0, 0.0).astype(BF)


INPUTS = ("w1", "w3", "k", "w2", "rate_row", "v", "g", "gain_row", "q")


def body(heads, toks, ins, outs, s):
    q_ref, k_ref, v_ref, g_ref, w1_ref, w3_ref, w2_ref = s.q, s.k, s.v, s.g, s.w1, s.w3, s.w2
    T, DH = q_ref.shape
    FH = w1_ref.shape[1]
    Z = toks // (CORES * XS)
    BR = DH * FH // (CORES * XS * LANE)
    NS = BR // Z
    fl, dl = Layout(FH, Z), Layout(DH, Z)
    layouts = (dl, fl, fl)
    JS = (FH // LANE, DH // LANE, DH // LANE)
    h = lax.axis_index("head")
    t = lax.axis_index("tok")
    c = lax.rem(t, CORES)
    x = lax.rem(t // CORES, XS)
    z = t // (CORES * XS)
    ZL = Z // QUADS
    QR = BR // QUADS
    q, zl = z // ZL, lax.rem(z, ZL)
    quad_order = sorted(range(QUADS), key=lambda k: (-min(k, QUADS - k), k))

    def quad(k):
        return lax.rem(q + k, QUADS)

    def at(c_, x_, z_):
        return (h, (z_ * XS + x_) * CORES + c_)

    other = at(1 - c, x, z)

    def x_peer(k):
        return lax.rem(x + k, XS)

    def z_peer(k):
        return lax.rem(z + k, Z)

    def head_peer(k):
        return lax.rem(h + k, heads)

    x_order = sorted(range(1, XS), key=lambda k: -min(k, XS - k))

    loads = {}
    for i, name in enumerate(INPUTS):
        loads[name] = pltpu.make_async_copy(ins[name], getattr(s, name), s.insem.at[i])

    barrier = pltpu.get_barrier_semaphore()
    near = [other] + [at(c, x_peer(k), z) for k in range(1, XS)]
    near += [at(c, x, z_peer(k)) for k in (1, Z - 1, 2, Z - 2)]
    near += [(head_peer(k), t) for k in range(1, heads)]
    for device in near:
        pl.semaphore_signal(barrier, inc=1, device_id=device, device_id_type=MESH)
    for name in INPUTS:
        loads[name].start()

    rounds = log2(Z) - 2

    def reach_signal(i):
        if i < rounds:
            for k in (2 * 2**i, Z - 2 * 2**i):
                pl.semaphore_signal(s.reach.at[i], inc=1, device_id=at(c, x, z_peer(k)), device_id_type=MESH)

    def reach_wait(i):
        if i < rounds:
            pl.semaphore_wait(s.reach.at[i], 2)

    RC = min(32, T)

    def each_rows(fn):
        def step(i, carry):
            fn(pl.ds(pl.multiple_of(i * RC, RC), RC))
            return carry

        lax.fori_loop(0, T // RC, step, 0)

    def remote(src, dst, send, recv, device):
        return pltpu.make_async_remote_copy(
            src_ref=src, dst_ref=dst, send_sem=send, recv_sem=recv, device_id=device, device_id_type=MESH
        )

    def wide(v, n):
        return jnp.concatenate([v] * (n // LANE), axis=1)

    def column(row):
        return jnp.broadcast_to(row, (LANE, row.shape[1])).T

    def parts(hidden):
        sg = jax.nn.sigmoid(hidden)
        return sg, hidden * sg, sg * (1.0 + hidden * (1.0 - sg))

    def put(ph, m, val):
        lay, js = layouts[m], JS[m]
        for cx in range(CORES * XS):
            for qq in range(QUADS):
                row = cx * lay.rows + qq * lay.quad
                for j in range(js):
                    lo = m * QR + j * lay.quad
                    s.sb[ph][cx // XS, qq, cx % XS, lo:lo + lay.quad, :] = val[
                        row:row + lay.quad, j * LANE:(j + 1) * LANE
                    ].astype(BF)

    def core_copy(ph, k):
        qq = quad(k)
        return remote(s.sb[ph].at[1 - c, qq], s.cr[ph].at[qq], s.sems.at[ph, 0, k], s.sems.at[ph, 1, k], other)

    def rs_core(ph):
        for k in quad_order:
            core_copy(ph, k).start()

    def rs_x(ph, k):
        qq = quad(k)
        sb, cr, xs, xr = s.sb[ph], s.cr[ph], s.xs[ph], s.xr[ph]
        core_copy(ph, k).wait_recv()
        for i in x_order:
            xd = x_peer(i)
            xs[qq, xd] = (sb[c, qq, xd].astype(F32) + cr[qq, xd].astype(F32)).astype(BF)
            remote(
                xs.at[qq, xd], xr.at[k, x], s.sems.at[ph, 2, k], s.sems.at[ph, 3, k], at(c, xd, z)
            ).start()
        s.acc[qq] = sb[c, qq, x].astype(F32) + cr[qq, x].astype(F32)

    def three(ref, ph, k):
        span = ref.at[k, pl.ds(0, XS - 1)]
        return remote(span, span, s.sems.at[ph, 2, k], s.sems.at[ph, 3, k], other)

    def rs_z(ph, k):
        qq = quad(k)
        xr, zs, zr = s.xr[ph], s.zs[ph], s.zr[ph]
        three(xr, ph, k).wait_recv()
        total = s.acc[qq]
        for i in range(1, XS):
            total = total + xr[k, x_peer(i)].astype(F32)
        total = jnp.concatenate([total[m * QR:(m + 1) * QR] for m in range(MATS)], axis=1).astype(BF)
        chunks = nn(s.perm[...], total)
        for m in range(MATS):
            zs[qq, :, m * NS:(m + 1) * NS, :] = chunks[:, m * LANE:(m + 1) * LANE].reshape(ZL, NS, LANE).astype(BF)
        for i in range(1, ZL) if k == 0 else range(ZL):
            ll = lax.rem(zl + i, ZL)
            remote(
                zs.at[qq, ll], zr.at[z], s.sems.at[ph, 4, 0], s.sems.at[ph, 5, 0], at(c, x, qq * ZL + ll)
            ).start()

    def rs_z_all(ph):
        span = s.zr[ph].at[pl.ds(0, Z - 1)]
        return remote(span, span, s.sems.at[ph, 4, 0], s.sems.at[ph, 5, 0], other)

    def rs_own(ph):
        rs_z_all(ph).wait_recv()
        total = s.zs[ph][q, zl].astype(F32)
        for k in range(1, Z):
            total = total + s.zr[ph][z_peer(k)].astype(F32)
        return [total[m * NS:(m + 1) * NS] for m in range(MATS)]

    def rs_drain(ph):
        for k in quad_order:
            core_copy(ph, k).wait_send()
            three(s.xr[ph], ph, k).wait_send()
        rs_z_all(ph).wait_send()

    def ag_z(ph, vals):
        ab, base = s.ab[ph], 3 + ph
        ab[c, q, x, zl] = jnp.concatenate(vals, axis=0).astype(BF)
        mine = ab.at[c, q, x, zl]
        for k in quad_order:
            for i in range(1, ZL) if k == 0 else range(ZL):
                ll = lax.rem(zl + i, ZL)
                remote(
                    mine, mine, s.sems.at[base, 4, k], s.sems.at[base, 5, (QUADS - k) % QUADS],
                    at(c, x, quad(k) * ZL + ll),
                ).start()

    def ag_z_quad(ph, k):
        n = ZL - 1 if k == 0 else ZL
        span = s.ab[ph].at[c, quad(k), x, pl.ds(0, n)]
        return remote(span, span, s.sems.at[3 + ph, 4, k], s.sems.at[3 + ph, 5, k], other)

    def ag_x(ph, k):
        base = 3 + ph
        ag_z_quad(ph, k).wait_recv()
        mine = s.ab[ph].at[c, quad(k), x]
        for i in x_order:
            remote(
                mine, mine, s.sems.at[base, 2, k], s.sems.at[base, 3, k], at(c, x_peer(i), z)
            ).start()

    def ag_x_quad(ph, k):
        span = s.ab[ph].at[c, quad(k), pl.ds(0, XS - 1)]
        return remote(span, span, s.sems.at[3 + ph, 2, k], s.sems.at[3 + ph, 3, k], other)

    def ag_core_quad(ph, k, cc):
        span = s.ab[ph].at[cc, quad(k)]
        return remote(span, span, s.sems.at[3 + ph, 0, k], s.sems.at[3 + ph, 1, k], other)

    def unpack(ph, cc, dst):
        for m in range(MATS):
            lay, js = layouts[m], JS[m]
            blocks = jnp.concatenate(
                [
                    s.ab[ph][cc, :, xx, :, m * NS:(m + 1) * NS, :].astype(F32).reshape(BR, LANE)
                    for xx in range(XS)
                ],
                axis=1,
            )
            rows = nn((s.permd if m == 0 else s.permf)[...], blocks.astype(BF)).astype(BF)
            for xx in range(XS):
                lo = pl.multiple_of((cc * XS + xx) * lay.rows, lay.rows)
                for j in range(js):
                    dst[m][pl.ds(lo, lay.rows), j * LANE:(j + 1) * LANE] = rows[
                        j * lay.rows:(j + 1) * lay.rows, xx * LANE:(xx + 1) * LANE
                    ]

    def gather(ph, vals, dst):
        ag_z(ph, vals)
        arrival = sorted(range(QUADS), key=lambda k: (min(k, QUADS - k), k))
        for k in arrival:
            ag_x(ph, k)
        for k in arrival:
            ag_x_quad(ph, k).wait_recv()
            ag_core_quad(ph, k, c).start()
        unpack(ph, c, dst)
        for k in arrival:
            ag_core_quad(ph, k, 1 - c).wait_recv()
        unpack(ph, 1 - c, dst)

    def ag_drain(ph):
        for k in quad_order:
            n = ZL - 1 if k == 0 else ZL
            span = s.ab[ph].at[c, q, x, pl.ds(0, n)]
            remote(span, span, s.sems.at[3 + ph, 4, k], s.sems.at[3 + ph, 5, k], other).wait_send()
            ag_x_quad(ph, k).wait_send()
            ag_core_quad(ph, k, c).wait_send()

    def colsum(val, r):
        total = jnp.broadcast_to(jnp.sum(val, axis=1, keepdims=True), (NS, LANE))
        shift = r
        while shift < NS:
            total = total + pltpu.roll(total, shift, 0)
            shift *= 2
        return total

    def put_down(val):
        high = val.astype(BF).astype(F32)
        middle = (val - high).astype(BF).astype(F32)
        low = val - high - middle
        split = jnp.concatenate([high, middle, low, jnp.zeros_like(low)], axis=0).astype(BF)
        total = None
        for j in range(JS[0]):
            part = nn(split, s.pft[j * LANE:(j + 1) * LANE, :])
            part = part[0:NS] + part[NS:2 * NS] + part[2 * NS:3 * NS]
            part = part[j * dl.r:(j + 1) * dl.r]
            total = part if total is None else total + part
        s.own0[...] = total

    def match(left, right):
        return jnp.where(left == right, 1.0, 0.0).astype(BF)

    small = (QR, QR)
    rows_i, cols_i = lax.broadcasted_iota(jnp.int32, small, 0), lax.broadcasted_iota(jnp.int32, small, 1)
    s.perm[...] = match(
        rows_i, ((cols_i & (ZL - 1)) << log2(NS)) | lax.shift_right_logical(cols_i, log2(ZL))
    )
    rows_i = lax.broadcasted_iota(jnp.int32, (BR, BR), 0)
    cols_i = lax.broadcasted_iota(jnp.int32, (BR, BR), 1)
    s.permd[...] = match(dl.chunk_row(rows_i, NS), cols_i)
    s.permf[...] = match(fl.chunk_row(rows_i, NS), cols_i)
    s.pft[...] = fl.onehot_t()
    w1t, w3t, w2t = s.w1t, s.w3t, s.w2t
    s.pd[...] = dl.onehot()
    loads["w1"].wait()
    w1t[...] = nt(s.pft[...], w1_ref[...]).astype(BF)
    loads["w3"].wait()
    w3t[...] = nt(s.pft[...], w3_ref[...]).astype(BF)

    loads["k"].wait()
    s.gp[...] = nt(k_ref[...], w1t[...])
    s.up[...] = nt(k_ref[...], w3t[...])

    def mix(rows):
        _, silu, _ = parts(s.gp[rows, :])
        s.mixed[rows, :] = (silu * s.up[rows, :]).astype(BF)

    each_rows(mix)
    loads["rate_row"].wait()
    s.rate[...] = column(s.rate_row[...])
    loads["v"].wait()

    def scale_v(rows):
        s.vn[rows, :] = (-wide(s.rate[rows, :], DH) * v_ref[rows, :].astype(F32)).astype(BF)

    each_rows(scale_v)
    s.vp[...] = nn(s.vn[...], s.pd[...]).astype(BF)
    put(0, 0, tn(s.vp[...], s.mixed[...]))
    loads["w2"].wait()
    w2t[...] = tn(nn(w2_ref[...], s.pd[...]).astype(BF), fl.onehot()).astype(BF)
    s.db[...] = nn(s.vp[...], w2t[...])

    def backs(rows):
        _, silu, slope = parts(s.gp[rows, :])
        db = s.db[rows, :]
        s.gb[rows, :] = (db * s.up[rows, :] * slope).astype(BF)
        s.ub[rows, :] = (db * silu).astype(BF)

    each_rows(backs)
    put(0, 1, tn(s.gb[...], k_ref[...]))
    pl.semaphore_wait(barrier, len(near))
    reach_signal(0)
    put(0, 2, tn(s.ub[...], k_ref[...]))
    rs_core(0)
    for i, k in enumerate(quad_order):
        rs_x(0, k)
        if i == 0:
            reach_wait(0)
            reach_signal(1)
    for i in range(1, rounds):
        reach_wait(i)
        reach_signal(i + 1)
    for k in quad_order:
        rs_z(0, k)

    priors = [None] * 3
    for m, wt in ((0, w2t), (1, w1t), (2, w3t)):
        lay, js = layouts[m], JS[m]
        lo = pl.multiple_of((c * XS + x) * lay.rows, lay.rows)
        block = jnp.concatenate(
            [wt[pl.ds(lo, lay.rows), j * LANE:(j + 1) * LANE] for j in range(js)], axis=0
        )
        s.prior[...] = tn((s.permd if m == 0 else s.permf)[...], block)
        priors[m] = s.prior[pl.ds(pl.multiple_of(z * NS, NS), NS), :]
    loads["gain_row"].wait()
    loads["g"].wait()
    loads["q"].wait()
    gain = s.gain_row[...]
    high = gain.astype(BF).astype(F32)
    middle = (gain - high).astype(BF).astype(F32)
    low = gain - high - middle
    row8 = lax.broadcasted_iota(jnp.int32, (8, DH), 0)
    split = jnp.where(row8 == 0, high, jnp.where(row8 == 1, middle, jnp.where(row8 == 2, low, 0.0)))
    gain_p = jnp.sum(nn(split.astype(BF), s.pd[...]), axis=0, keepdims=True)
    s.gw[...] = nn(g_ref[...], s.pd[...]) * gain_p

    moved, prior_norm, moved_norm = [None] * 3, [None] * 3, [None] * 3
    for m in range(3):
        prior_norm[m] = jnp.sqrt(colsum(priors[m] * priors[m], layouts[m].r) + EPSILON)
    got = rs_own(0)
    fast = []
    for m in range(MATS):
        moved[m] = priors[m] - got[m]
        moved_norm[m] = jnp.sqrt(colsum(moved[m] * moved[m], layouts[m].r) + EPSILON)
        fast.append(moved[m] * (prior_norm[m] / moved_norm[m]))
    f1t, f3t, f2t = s.f1t, s.f3t, s.f2t
    gather(0, fast, (f2t, f1t, f3t))

    s.qg[...] = nt(q_ref[...], f1t[...])
    s.qu[...] = nt(q_ref[...], f3t[...])

    def qmix(rows):
        _, silu, _ = parts(s.qg[rows, :])
        s.qm[rows, :] = (silu * s.qu[rows, :]).astype(BF)

    each_rows(qmix)
    s.out[...] = nt(s.qm[...], f2t[...])

    def fold(rows):
        o, w = s.out[rows, :], s.gw[rows, :]
        sq, dt = o * o, w * o
        s.sq[rows, :] = sum(sq[:, j * LANE:(j + 1) * LANE] for j in range(DH // LANE))
        s.dt[rows, :] = sum(dt[:, j * LANE:(j + 1) * LANE] for j in range(DH // LANE))

    each_rows(fold)
    row_sq = jnp.sum(s.sq[...].T, axis=0, keepdims=True)
    row_dt = jnp.sum(s.dt[...].T, axis=0, keepdims=True)
    row8t = lax.broadcasted_iota(jnp.int32, (8, T), 0)
    s.hs[...] = jnp.where(row8t == 0, row_sq, row_dt)
    for k in range(1, heads):
        remote(s.hs, s.hr.at[h], s.hsem.at[0], s.hsem.at[1], (head_peer(k), t)).start()
    span = s.hr.at[pl.ds(0, heads - 1)]
    remote(span, span, s.hsem.at[0], s.hsem.at[1], other).wait_recv()
    both = s.hs[...]
    for k in range(1, heads):
        both = both + s.hr[head_peer(k)]
    full_width = heads * DH
    square, dots = both[0:1], both[1:2]
    inverse = lax.rsqrt(square / full_width + EPSILON)
    s.inv[...] = column(inverse)
    s.coef[...] = column(inverse * inverse * inverse * dots / full_width)

    def outback(rows):
        s.ob[rows, :] = (
            wide(s.inv[rows, :], DH) * s.gw[rows, :] - s.out[rows, :] * wide(s.coef[rows, :], DH)
        ).astype(BF)

    each_rows(outback)

    put(1, 0, tn(s.ob[...], s.qm[...]))
    s.qb[...] = nn(s.ob[...], f2t[...])

    def qbacks(rows):
        _, silu, slope = parts(s.qg[rows, :])
        qb = s.qb[rows, :]
        s.qgb[rows, :] = (qb * s.qu[rows, :] * slope).astype(BF)
        s.qub[rows, :] = (qb * silu).astype(BF)

    each_rows(qbacks)
    put(1, 1, tn(s.qgb[...], q_ref[...]))
    put(1, 2, tn(s.qub[...], q_ref[...]))
    rs_core(1)
    for k in quad_order:
        rs_x(1, k)
    for k in quad_order:
        rs_z(1, k)
    s.qo[...] = (nn(s.qgb[...], f1t[...]) + nn(s.qub[...], f3t[...])).astype(BF)
    stores = [pltpu.make_async_copy(s.qo, outs[0], s.outsem.at[0])]
    stores[0].start()

    owned = [None] * 3
    got = rs_own(1)
    cot = []
    for m in range(MATS):
        grad, mn, pn = got[m], moved_norm[m], prior_norm[m]
        dot = colsum(grad * moved[m], layouts[m].r)
        moved_grad = pn / mn * (grad - moved[m] * (dot / (mn * mn)))
        owned[m] = moved_grad + priors[m] * (dot / (mn * pn))
        cot.append(moved_grad)
    c1t, c3t, c2t = s.c1t, s.c3t, s.c2t
    gather(1, cot, (c2t, c1t, c3t))

    s.qg[...] = nt(k_ref[...], c1t[...])
    s.qu[...] = nt(k_ref[...], c3t[...])
    s.qb[...] = nn(s.vp[...], c2t[...])

    def bars(rows):
        hidden, up, db = s.gp[rows, :], s.up[rows, :], s.db[rows, :]
        gate_bar, up_bar, mixed_bar = s.qg[rows, :], s.qu[rows, :], s.qb[rows, :]
        sg, silu, slope = parts(hidden)
        curve = sg * (1.0 - sg) * (2.0 + hidden * (1.0 - 2.0 * sg))
        s.dbb[rows, :] = (gate_bar * up * slope + up_bar * silu).astype(BF)
        s.qub[rows, :] = (gate_bar * db * slope + mixed_bar * silu).astype(BF)
        s.qgb[rows, :] = ((up_bar * db + mixed_bar * up) * slope + gate_bar * db * up * curve).astype(BF)

    each_rows(bars)
    put(2, 0, tn(s.vp[...], s.dbb[...]))
    put(2, 1, tn(s.qgb[...], k_ref[...]))
    put(2, 2, tn(s.qub[...], k_ref[...]))
    rs_core(2)
    for k in quad_order:
        rs_x(2, k)
    for k in quad_order:
        rs_z(2, k)

    s.out[...] = nt(s.mixed[...], c2t[...]) + nt(s.dbb[...], w2t[...])

    def value(rows):
        s.vn[rows, :] = (wide(s.rate[rows, :], DH) * s.out[rows, :]).astype(BF)

    each_rows(value)
    s.vo[...] = nt(s.vn[...], s.pd[...]).astype(BF)
    stores.append(pltpu.make_async_copy(s.vo, outs[2], s.outsem.at[1]))
    stores[1].start()
    s.ko[...] = (
        -(nn(s.gb[...], c1t[...]) + nn(s.ub[...], c3t[...]) + nn(s.qgb[...], w1t[...]) + nn(s.qub[...], w3t[...]))
    ).astype(BF)
    stores.append(pltpu.make_async_copy(s.ko, outs[1], s.outsem.at[2]))
    stores[2].start()

    got = rs_own(2)
    for m in range(MATS):
        final = owned[m] - got[m]
        if m == 0:
            put_down(final)
            stores.append(pltpu.make_async_copy(s.own0, outs[3], s.outsem.at[3]))
        else:
            own = (s.own1, s.own2)[m - 1]
            own[...] = final
            stores.append(pltpu.make_async_copy(own, outs[3 + m], s.outsem.at[3 + m]))
        stores[-1].start()
    for ph in range(3):
        rs_drain(ph)
    for ph in range(2):
        ag_drain(ph)
    hall = s.hr.at[pl.ds(0, heads - 1)]
    remote(hall, hall, s.hsem.at[0], s.hsem.at[1], other).wait_send()
    for store in stores:
        store.wait()


class Scratch:
    def __init__(self, heads, toks, T, DH, FH):
        self.specs, self.names = [], []
        Z = toks // (CORES * XS)
        BR = DH * FH // (CORES * XS * LANE)
        NS = BR // Z

        def vm(name, *shape, dtype=BF):
            self.specs.append(pltpu.VMEM(shape, dtype))
            self.names.append(name)

        for name in ("gp", "up", "db", "qg", "qu", "qb"):
            vm(name, T, FH, dtype=F32)
        for name in ("mixed", "gb", "ub", "qm", "qgb", "qub", "dbb"):
            vm(name, T, FH)
        for name in ("vn", "vp", "ob"):
            vm(name, T, DH)
        for name in ("gw", "out"):
            vm(name, T, DH, dtype=F32)
        for name in ("rate", "inv", "coef", "sq", "dt"):
            vm(name, T, LANE, dtype=F32)
        for name in ("w1t", "w3t", "f1t", "f3t", "c1t", "c3t"):
            vm(name, FH, DH)
        for name in ("w2t", "f2t", "c2t"):
            vm(name, DH, FH)
        for name in ("q", "k", "v", "g", "qo", "ko", "vo"):
            vm(name, T, DH)
        vm("w1", DH, FH)
        vm("w3", DH, FH)
        vm("w2", FH, DH)
        vm("rate_row", 1, T, dtype=F32)
        vm("gain_row", 1, DH, dtype=F32)
        vm("own0", Layout(DH, Z).r, FH, dtype=F32)
        vm("own1", NS, LANE, dtype=F32)
        vm("own2", NS, LANE, dtype=F32)
        vm("pft", FH, FH)
        vm("pd", DH, DH)
        QR, ZL = BR // QUADS, Z // QUADS
        vm("perm", QR, QR)
        vm("permd", BR, BR)
        vm("permf", BR, BR)
        vm("prior", BR, LANE, dtype=F32)
        vm("hs", 8, T, dtype=F32)
        vm("hr", heads, 8, T, dtype=F32)
        vm("acc", QUADS, MATS * QR, LANE, dtype=F32)
        for ph in range(3):
            vm(("sb", ph), CORES, QUADS, XS, MATS * QR, LANE)
            vm(("cr", ph), QUADS, XS, MATS * QR, LANE)
            vm(("xs", ph), QUADS, XS, MATS * QR, LANE)
            vm(("xr", ph), QUADS, XS, MATS * QR, LANE)
            vm(("zs", ph), QUADS, ZL, MATS * NS, LANE)
            vm(("zr", ph), Z, MATS * NS, LANE)
        for ph in range(2):
            vm(("ab", ph), CORES, QUADS, XS, ZL, MATS * NS, LANE)
        for name, shape in (
            ("sems", (5, 6, QUADS)), ("hsem", (2,)), ("insem", (len(INPUTS),)), ("outsem", (6,))
        ):
            self.specs.append(pltpu.SemaphoreType.DMA(shape))
            self.names.append(name)
        self.specs.append(pltpu.SemaphoreType.REGULAR((max(1, log2(Z) - 2),)))
        self.names.append("reach")

    def bind(self, refs):
        class Refs:
            pass

        s = Refs()
        for name, ref in zip(self.names, refs):
            if isinstance(name, str):
                setattr(s, name, ref)
            else:
                held = getattr(s, name[0], [])
                held.append(ref)
                setattr(s, name[0], held)
        return s


def per_device(heads, toks, query, key, value, out_grad, rates, gain, w1, w3, w2):
    T, DH = query.shape
    FH = w1.shape[2]
    Z = toks // (CORES * XS)
    NS = DH * FH // (CORES * XS * LANE) // Z
    scratch = Scratch(heads, toks, T, DH, FH)

    arrays = dict(
        q=query, k=key, v=value, g=out_grad, rate_row=rates.reshape(1, T), gain_row=gain.reshape(1, DH),
        w1=w1[0], w3=w3[0], w2=w2[0],
    )

    def kernel(*refs):
        n = len(INPUTS)
        body(heads, toks, dict(zip(INPUTS, refs[:n])), refs[n:n + 6], scratch.bind(refs[n + 6:]))

    anywhere, hbm = pl.BlockSpec(memory_space=pl.ANY), pl.BlockSpec(memory_space=pltpu.HBM)
    tokens = jax.ShapeDtypeStruct((T, DH), BF)
    fr, dr = Layout(FH, Z).r, Layout(DH, Z).r
    columns = jax.ShapeDtypeStruct((NS, LANE), F32)
    shapes = (tokens, tokens, tokens, jax.ShapeDtypeStruct((dr, FH), F32), columns, columns)
    results = pl.pallas_call(
        kernel,
        out_shape=shapes,
        in_specs=[hbm] * len(INPUTS),
        out_specs=(anywhere,) * 6,
        scratch_shapes=scratch.specs,
        compiler_params=pltpu.CompilerParams(
            collective_id=0, has_side_effects=True, vmem_limit_bytes=VMEM_LIMIT
        ),
        name="lact_backward",
    )(*(pltpu.with_memory_space_constraint(arrays[name], pltpu.HBM) for name in INPUTS))

    def hand_on(*refs):
        sems = refs[12]
        copies = [pltpu.make_async_copy(refs[i], refs[6 + i], sems.at[i]) for i in range(6)]
        for copy in copies:
            copy.start()
        for copy in copies:
            copy.wait()

    qo, ko, vo, down, gate, up = pl.pallas_call(
        hand_on,
        out_shape=shapes,
        in_specs=[anywhere] * 6,
        out_specs=(hbm,) * 6,
        scratch_shapes=[pltpu.SemaphoreType.DMA((6,))],
        compiler_params=pltpu.CompilerParams(vmem_limit_bytes=1024 * 1024),
        name="hand_on",
    )(*results)
    down = down.T.reshape(1, FH, dr)
    gate = gate.reshape(DH // LANE, fr, LANE).transpose(0, 2, 1).reshape(1, DH, fr)
    up = up.reshape(DH // LANE, fr, LANE).transpose(0, 2, 1).reshape(1, DH, fr)
    return qo, ko, vo, gate, up, down


def solution(mesh):
    heads, toks = mesh.shape["head"], mesh.shape["tok"]
    token_spec, weight_in, weight_out = P("tok", "head"), P("head", None, None), P("head", None, "tok")

    def step(*args):
        return per_device(heads, toks, *args)

    return jax.shard_map(
        step,
        mesh=mesh,
        in_specs=(token_spec,) * 5 + (P("head"),) + (weight_in,) * 3,
        out_specs=(token_spec,) * 3 + (weight_out,) * 3,
        check_vma=False,
    )
```
